32 devices in a mesh: groups: 2 (over y), queue: 8 (over z, x), tp: 2 (over core).
Axes of the slice: x: 2, y: 2, z: 4, core: 2. Of those that a mesh axis runs over, the one named last changes fastest.
Arguments:
- hidden: bfloat16 [3328, 5120], P(('groups', 'queue'), 'tp'), parts along dimension 0, may hold values from -8 to 8
- q_weight: bfloat16 [1, 40, 128, 128], P(None, 'tp'), may hold values from -1 to 2.5
- k_weight: bfloat16 [1, 40, 128, 128], P(None, 'tp'), may hold values from -1 to 2.5
- v_weight: bfloat16 [1, 40, 128, 128], P(None, 'tp'), may hold values from -0.5 to 0.5
- mod_base: float32 [1, 3, 5120], P(None, None, 'tp'), may hold values from -3 to 3
- mod_amp: float32 [1, 3, 5120], P(None, None, 'tp'), may hold values from -3 to 3
- levels: int32 [16], P(('groups', 'queue')), parts along dimension 0, may hold values from 0 to 63
- steps_table: int32 [65], replicated, may hold values from 0 to 1000
- group_pos: int32 [16], P('groups'), parts along dimension 0, may hold values from 0 to 31
Outputs:
- new_queue: bfloat16 [3328, 5120], P(('groups', 'queue'), 'tp'), parts along dimension 0
- velocity: bfloat16 [3328, 5120], P(('groups', 'queue'), 'tp'), parts along dimension 0
The draws below stay inside these ranges and needn't reach their ends.
There are 2 independent parts, one for each index of `groups`. The reference program is written for one: setup_inputs(seed, part) draws one part's arguments, and reference() takes and returns one part's arrays. A program takes and returns all parts, laid end to end along the dimension named above; an argument that names none is the same for every part. Nothing has to cross between parts.
All inputs are finite; a program needn't handle non-finite values.
Results may differ from the reference program's by a relative error of at most 0.0054.
Values may be sent and summed in bfloat16 or wider, within the bound.
No kernel may reach another device: no remote copies, remote signals or barrier semaphores. Data moves between devices by JAX's collectives and lax.ppermute only.
A program may use at most 64 MiB of HBM per device.

```python
import math
import jax
import jax.numpy as jnp
from jax import lax

HEADS = 40
HEAD = 128
D = 5120
WIDE = 52
HW_DEV = 104
TOK_DEV = 208
BLOCKS = 1
STEPS = 64
QUEUE = 8
TOKENS = 1664


def draw_hidden(key, part):
    keys = jax.random.split(jax.random.fold_in(key, 11), 1)
    result = jnp.clip(jax.random.normal(keys[0], (TOKENS, D), jnp.float32), -6.0, 6.0)
    return result.astype(jnp.bfloat16)


def head_map(key):
    noise = jnp.clip(jax.random.normal(key, (BLOCKS, HEADS, HEAD, HEAD), jnp.float32), -6.0, 6.0)
    diag = 0.3
    noise = noise / jnp.sqrt(jnp.float32(HEAD))
    ident = jnp.eye(HEAD, dtype=jnp.float32)
    return (noise + diag * ident[None, None]).astype(jnp.bfloat16)


def draw_q_weight(key, part):
    return head_map(jax.random.fold_in(key, 23))


def draw_k_weight(key, part):
    return head_map(jax.random.fold_in(key, 37))


def with_ends(values, key, low, largest):
    spot = [jax.random.randint(jax.random.fold_in(key, axis), (), 0, length) for axis, length in enumerate(values.shape)]
    widest = values.shape.index(max(values.shape))
    neighbour = spot[:widest] + [(spot[widest] + 1) % values.shape[widest]] + spot[widest + 1:]
    return values.at[tuple(spot)].set(low).at[tuple(neighbour)].set(largest)


def block_levels(own_key, extent, pieces, smallest, largest):
    def one(dim, blocks):
        steps = jax.random.uniform(jax.random.fold_in(jax.random.fold_in(own_key, 6), dim), (blocks,), jnp.float32, smallest / len(pieces), largest / len(pieces))
        return jnp.repeat(jnp.exp(steps), extent[dim] // blocks).reshape((-1,) + (1,) * (len(extent) - dim - 1))

    factor_of = one(*pieces[0])
    for cut in pieces[1:]:
        factor_of = factor_of * one(*cut)
    return factor_of


def gaussian(key, dims, deviation, reach, cuts=(), kind=jnp.bfloat16):
    drawn = deviation * jax.random.normal(key, dims, jnp.float32)
    if cuts:
        drawn = drawn * block_levels(key, dims, cuts, -0.22, 0.18)
    return jnp.clip(drawn, -reach, reach).astype(kind)


def setup_inputs(seed: int = 0, part: int = 0) -> dict:
    streams_of = jax.random.split(jax.random.key(seed), 10)
    part_keys = jax.random.split(jax.random.fold_in(streams_of[9], part), 10)
    return {
        "hidden": draw_hidden(jax.random.fold_in(jax.random.fold_in(streams_of[9], part), 71), part),
        "q_weight": draw_q_weight(jax.random.fold_in(streams_of[9], 71), part),
        "k_weight": draw_k_weight(jax.random.fold_in(streams_of[9], 71), part),
        "v_weight": gaussian(streams_of[3], (BLOCKS, HEADS, HEAD, HEAD), HEAD ** -0.5, 0.5, ((1, 2),)),
        "mod_base": gaussian(streams_of[4], (BLOCKS, 3, D), 0.5, 3.0, ((2, 2),), jnp.float32),
        "mod_amp": gaussian(streams_of[5], (BLOCKS, 3, D), 0.5, 3.0, ((2, 2),), jnp.float32),
        "levels": with_ends(jax.random.randint(part_keys[6], (QUEUE,), 0, STEPS), jax.random.fold_in(part_keys[6], 1), 0, STEPS - 1).astype(jnp.int32),
        "steps_table": with_ends(jax.random.randint(streams_of[7], (STEPS + 1,), 0, 1001), jax.random.fold_in(streams_of[7], 1), 0, 1000).astype(jnp.int32),
        "group_pos": with_ends(jax.random.randint(part_keys[8], (QUEUE,), 0, 4 * QUEUE), jax.random.fold_in(part_keys[8], 1), 0, (4 * QUEUE) - 1).astype(jnp.int32),
    }


def time_embed(moment, channel):
    within = channel % 256
    freq = jnp.exp(-jnp.log(10000.0) * (within % 128).astype(jnp.float32) / 128.0)
    angle = moment * freq
    return jnp.where(within < 128, jnp.cos(angle), jnp.sin(angle))

def angle_table(start, count):
    place = jnp.arange(count, dtype=jnp.int32)
    tpos = (start + place // HW_DEV).astype(jnp.float32)
    inner = place % HW_DEV
    hpos = (inner // WIDE).astype(jnp.float32)
    wpos = (inner % WIDE).astype(jnp.float32)
    side_pairs = HEAD // 6
    time_pairs = (HEAD - 4 * side_pairs) // 2
    freq_t = 10000.0 ** (-jnp.arange(time_pairs, dtype=jnp.float32) / time_pairs)
    freq_s = 10000.0 ** (-jnp.arange(side_pairs, dtype=jnp.float32) / side_pairs)
    return jnp.concatenate([tpos[:, None] * freq_t, hpos[:, None] * freq_s, wpos[:, None] * freq_s], axis=1)

def rotate(values, angles):
    count, heads, size = values.shape
    paired = values.reshape(count, heads, size // 2, 2)
    cosine = jnp.cos(angles)[:, None, :]
    sine = jnp.sin(angles)[:, None, :]
    first = paired[..., 0]
    second = paired[..., 1]
    turned = jnp.stack([first * cosine - second * sine, first * sine + second * cosine], axis=-1)
    return turned.reshape(count, heads, size)

def rms_rotate(raw, angles):
    total = lax.optimization_barrier(jnp.sum(raw * raw, axis=(1, 2)))
    scaled = raw * lax.rsqrt(total / D + 1e-06)[:, None, None]
    return rotate(scaled, angles).astype(jnp.bfloat16)

def attend_blocks(query, keys, values, valid, scale):
    count, heads, size = query.shape
    span = math.gcd(heads, 4)
    number = heads // span

    def one(block_index):
        qpart = lax.dynamic_slice_in_dim(query, block_index * span, span, 1).astype(jnp.float32)
        kpart = lax.dynamic_slice_in_dim(keys, block_index * span, span, 1).astype(jnp.float32)
        vpart = lax.dynamic_slice_in_dim(values, block_index * span, span, 1).astype(jnp.float32)
        scores = jnp.einsum('qhd,khd->hqk', qpart, kpart) * scale
        scores = jnp.where(valid[None, None, :], scores, jnp.float32(-1e+30))
        top = lax.optimization_barrier(jnp.max(scores, axis=-1, keepdims=True))
        expo = jnp.exp(scores - top)
        weights = (expo / lax.optimization_barrier(jnp.sum(expo, axis=-1, keepdims=True))).astype(jnp.bfloat16)
        return jnp.einsum('hqk,khd->qhd', weights.astype(jnp.float32), vpart)
    parts = lax.map(one, jnp.arange(number, dtype=jnp.int32))
    return jnp.transpose(parts, (1, 0, 2, 3)).reshape(count, heads * size)

def reference(hidden, q_weight, k_weight, v_weight, mod_base, mod_amp, levels, steps_table, group_pos):
    groups = hidden.reshape(QUEUE, TOK_DEV, D)
    state = groups.astype(jnp.float32)
    t_now = steps_table[levels].astype(jnp.float32)
    t_next = steps_table[levels + 1].astype(jnp.float32)
    channel = jnp.arange(D, dtype=jnp.int32)
    emb = time_embed(t_now[:, None], channel[None, :])
    scale = 1.0 / jnp.sqrt(jnp.float32(HEAD))
    for block in range(BLOCKS):
        mods = mod_base[block][None] + mod_amp[block][None] * emb[:, None, :]
        mean = lax.optimization_barrier(jnp.sum(state, axis=-1, keepdims=True)) / D
        second = lax.optimization_barrier(jnp.sum(state * state, axis=-1, keepdims=True)) / D
        normed = (state - mean) * lax.rsqrt(second - mean * mean + 1e-06)
        mixed = (normed * (1.0 + mods[:, 1:2, :]) + mods[:, 0:1, :]).astype(jnp.bfloat16)
        q_now = q_weight[block].astype(jnp.float32)
        k_now = k_weight[block].astype(jnp.float32)
        v_now = v_weight[block].astype(jnp.float32)

        def project(index):
            heads_here = mixed[index].reshape(TOK_DEV, HEADS, HEAD).astype(jnp.float32)
            angles = angle_table(group_pos[index], TOK_DEV)
            key_raw = jnp.einsum('thd,hde->the', heads_here, k_now)
            value = jnp.einsum('thd,hde->the', heads_here, v_now).astype(jnp.bfloat16)
            return (rms_rotate(key_raw, angles), value)
        all_keys, all_values = lax.map(project, jnp.arange(QUEUE, dtype=jnp.int32))

        def attend(index):
            before_index = jnp.maximum(index - 1, 0)
            after_index = jnp.minimum(index + 1, QUEUE - 1)
            own_heads = mixed[index].reshape(TOK_DEV, HEADS, HEAD).astype(jnp.float32)
            query_raw = jnp.einsum('thd,hde->the', own_heads, q_now)
            query = rms_rotate(query_raw, angle_table(group_pos[index], TOK_DEV))
            keys = jnp.concatenate([all_keys[before_index], all_keys[index], all_keys[after_index]], axis=0)
            values = jnp.concatenate([all_values[before_index], all_values[index], all_values[after_index]], axis=0)
            valid = jnp.concatenate([jnp.full((TOK_DEV,), index > 0), jnp.full((TOK_DEV,), True), jnp.full((TOK_DEV,), index < QUEUE - 1)])
            return attend_blocks(query, keys, values, valid, scale)
        attention = lax.map(attend, jnp.arange(QUEUE, dtype=jnp.int32))
        state = state + mods[:, 2:3, :] * attention
    velocity = state.astype(jnp.bfloat16)
    step_size = (t_next - t_now) / 1000.0
    advanced = (groups.astype(jnp.float32) + step_size[:, None, None] * state).astype(jnp.bfloat16)
    new_queue = jnp.concatenate([jnp.zeros((1, TOK_DEV, D), jnp.bfloat16), advanced[:-1]], axis=0)
    return (new_queue.reshape(TOKENS, D), velocity.reshape(TOKENS, D))
```

```python
import functools
import math

import jax
import jax.numpy as jnp
from jax import lax
from jax.experimental import pallas as pl
from jax.experimental.pallas import tpu as pltpu
from jax.sharding import PartitionSpec as P

WIDE = 52
HW_DEV = 104
PERIOD = 256
CHUNKS = 2
STEP_HEADS = 2
SUM_HEADS = 4
LIMIT = 24 << 20
F32 = jnp.float32
BF16 = jnp.bfloat16
VMEM = pl.BlockSpec(memory_space=pltpu.VMEM)


def send(array, pairs, length, wrap=False):
    if wrap:
        pairs = [(a, b % length) for a, b in pairs]
    pairs = [(a, b) for a, b in pairs if 0 <= b < length]
    return lax.ppermute(array, "queue", pairs)


def other_core(array):
    if lax.axis_size("tp") == 2:
        return lax.ppermute(array, "tp", [(0, 1), (1, 0)])
    return lax.psum(array, "tp") - array


def divisor(count, most):
    return max(k for k in range(1, most + 1) if count % k == 0)


def time_embed(moment, channel):
    within = channel % 256
    freq = jnp.exp(-jnp.log(10000.0) * (within % 128).astype(F32) / 128.0)
    angle = moment * freq
    return jnp.where(within < 128, jnp.cos(angle), jnp.sin(angle))


def pair_plan(shape, size):
    half = size // 2
    side = size // 6
    lead = (size - 4 * side) // 2
    pair = lax.broadcasted_iota(jnp.int32, shape, len(shape) - 1) % half
    part = jnp.where(pair < lead, 0, jnp.where(pair < lead + side, 1, 2))
    within = pair - jnp.where(part == 0, 0, jnp.where(part == 1, lead, lead + side))
    pairs = jnp.where(part == 0, lead, side).astype(F32)
    return part, jnp.exp(-math.log(10000.0) * (within.astype(F32) / pairs))


def pairs_apart(size):
    row = jnp.arange(size)[:, None]
    col = jnp.arange(size)[None, :]
    half = size // 2
    return (row == 2 * (col % half) + col // half).astype(BF16)


def normed_mix(x, mean, rstd, shift, scale):
    return ((x - mean) * rstd * (1.0 + scale) + shift).astype(BF16)


def to_rows(columns, size):
    count = columns[0].shape[0]
    lane = lax.broadcasted_iota(jnp.int32, (count, size), 1)
    wide = jnp.zeros((count, size), F32)
    for j, column in enumerate(columns):
        wide = jnp.where(lane == j, jnp.broadcast_to(column, (count, size)), wide)
    return jnp.transpose(wide)[:8]


def split_kernel(size, cuts, x_ref, *outs):
    out_ref = outs[-1]
    count, _ = x_ref.shape
    total = jnp.zeros((count, size), F32)
    second = jnp.zeros((count, size), F32)
    for piece, lo, hi in zip(outs, cuts[:-1], cuts[1:]):
        for h in range(lo, hi):
            raw = x_ref[:, h * size : (h + 1) * size]
            piece[:, (h - lo) * size : (h - lo + 1) * size] = raw
            x = raw.astype(F32)
            total += x
            second += x * x
    out_ref[...] = to_rows(
        [jnp.sum(total, axis=1, keepdims=True), jnp.sum(second, axis=1, keepdims=True)], size
    )


def split(x, cuts, size):
    count, width = x.shape
    return pl.pallas_call(
        functools.partial(split_kernel, size, cuts),
        name="token_split",
        in_specs=[VMEM],
        out_specs=[VMEM] * len(cuts),
        out_shape=[jax.ShapeDtypeStruct((count, (hi - lo) * size), BF16) for lo, hi in zip(cuts[:-1], cuts[1:])]
        + [jax.ShapeDtypeStruct((8, count), F32)],
        compiler_params=pltpu.CompilerParams(vmem_limit_bytes=LIMIT),
        cost_estimate=pl.CostEstimate(flops=4 * count * width, bytes_accessed=4 * count * width, transcendentals=0),
    )(x)


def squares_kernel(
    heads, size, width, level_ref, steps_ref,
    x_ref, own_ref, peer_ref, base_ref, amp_ref, q_ref, k_ref, out_ref, acc, tab, emb,
):
    count = x_ref.shape[0]

    @pl.when(pl.program_id(0) == 0)
    def _():
        acc[...] = jnp.zeros_like(acc)
        cols = jnp.transpose(own_ref[...] + peer_ref[...])
        mean = cols[:, 0:1] / width
        rstd = lax.rsqrt(cols[:, 1:2] / width - mean * mean + 1e-06)
        tab[0] = jnp.broadcast_to(mean, (count, size))
        tab[1] = jnp.broadcast_to(rstd, (count, size))
        t_now = steps_ref[level_ref[0]].astype(F32)
        first = lax.axis_index("tp") * (width // lax.axis_size("tp"))
        emb[...] = time_embed(t_now, lax.broadcasted_iota(jnp.int32, emb.shape, 1) + first)

    for h in range(heads):
        cut = slice(h * size, (h + 1) * size)
        off = (h * size) % PERIOD
        mod = lambda i: base_ref[i, :, cut] + amp_ref[i, :, cut] * emb[0:1, off : off + size]
        x = x_ref[:, cut].astype(F32)
        mixed = normed_mix(x, tab[0], tab[1], mod(0), mod(1))
        both = jnp.concatenate([q_ref[0, h], k_ref[0, h]], axis=1)
        raw = jnp.dot(mixed, both, preferred_element_type=F32)
        acc[...] += raw * raw

    @pl.when(pl.program_id(0) == pl.num_programs(0) - 1)
    def _():
        fill = lambda i: jnp.full((count, 1), steps_ref[level_ref[0] + i].astype(F32))
        out_ref[...] = to_rows(
            [
                tab[0][:, 0:1],
                tab[1][:, 0:1],
                jnp.sum(acc[:, :size], axis=1, keepdims=True),
                jnp.sum(acc[:, size:], axis=1, keepdims=True),
                fill(0),
                fill(1),
            ],
            size,
        )


def token_squares(x, own, peer, levels, steps_table, base, amp, q_weight, k_weight, width):
    count = x.shape[0]
    local_heads, size = q_weight.shape[1], q_weight.shape[2]
    heads = divisor(local_heads, SUM_HEADS)
    tokens = pl.BlockSpec((count, heads * size), lambda i, *_: (0, i))
    modspec = pl.BlockSpec((base.shape[0], 1, heads * size), lambda i, *_: (0, 0, i))
    weight = pl.BlockSpec((1, heads, size, size), lambda i, *_: (0, i, 0, 0))
    return pl.pallas_call(
        functools.partial(squares_kernel, heads, size, width),
        name="token_squares",
        grid_spec=pltpu.PrefetchScalarGridSpec(
            num_scalar_prefetch=2,
            grid=(local_heads // heads,),
            in_specs=[tokens, VMEM, VMEM, modspec, modspec, weight, weight],
            out_specs=pl.BlockSpec((8, count), lambda i, *_: (0, 0)),
            scratch_shapes=[
                pltpu.VMEM((count, 2 * size), F32),
                pltpu.VMEM((2, count, size), F32),
                pltpu.VMEM((8, PERIOD), F32),
            ],
        ),
        out_shape=jax.ShapeDtypeStruct((8, count), F32),
        compiler_params=pltpu.CompilerParams(dimension_semantics=("arbitrary",), vmem_limit_bytes=LIMIT),
        cost_estimate=pl.CostEstimate(
            flops=4 * count * local_heads * size * size,
            bytes_accessed=2 * count * local_heads * size + 4 * local_heads * size * size,
            transcendentals=0,
        ),
    )(levels, steps_table, x, own, peer, base, amp, q_weight, k_weight)


def tables_kernel(
    first, pos_ref, a_ref, b_ref, c_ref, d_ref,
    mean_ref, rstd_ref, ck_ref, sk_ref, cq_ref, sq_ref, emb_ref, step_ref,
):
    count, size = mean_ref.shape[1:]
    frames = -(-count // HW_DEV)
    position = lax.axis_index("queue")
    last = lax.axis_size("queue") - 1
    inner = lax.broadcasted_iota(jnp.int32, (HW_DEV, size), 0)
    part, freq = pair_plan((HW_DEV, size), size)
    hpos = (inner // WIDE).astype(F32)
    wpos = (inner % WIDE).astype(F32)
    angle = jnp.where(part == 1, hpos, wpos) * freq
    pcos, psin = jnp.cos(angle), jnp.sin(angle)
    row = lax.broadcasted_iota(jnp.int32, (8, size), 0)
    _, ffreq = pair_plan((8, size), size)
    sign = jnp.where(lax.broadcasted_iota(jnp.int32, (1, size), 1) < size // 2, -1.0, 1.0)
    emb_row = lax.broadcasted_iota(jnp.int32, emb_ref.shape, 0)
    moment = jnp.zeros(emb_ref.shape, F32)
    for g, stats in enumerate((a_ref, b_ref, c_ref, d_ref)):
        start = pos_ref[jnp.clip(position + (g - 2), 0, last)]
        fangle = (start + row).astype(F32) * ffreq
        fcos, fsin = jnp.cos(fangle), jnp.sin(fangle)
        cols = jnp.transpose(stats[...])
        moment = jnp.where(emb_row == g, stats[4:5, 0:1], moment)
        for f in range(frames):
            lo, hi = f * HW_DEV, min((f + 1) * HW_DEV, count)
            cos = jnp.where(part == 0, fcos[f : f + 1], pcos)[: hi - lo]
            sin = jnp.where(part == 0, fsin[f : f + 1], psin)[: hi - lo] * sign
            column = lambda j: jnp.broadcast_to(cols[lo:hi, j : j + 1], (hi - lo, size))
            mean_ref[g, lo:hi] = column(0)
            rstd_ref[g, lo:hi] = column(1)
            ck_ref[g, lo:hi] = cos * column(3)
            sk_ref[g, lo:hi] = sin * column(3)
            if g in (1, 2):
                cq_ref[g - 1, lo:hi] = cos * column(2)
                sq_ref[g - 1, lo:hi] = sin * column(2)
    channel = lax.broadcasted_iota(jnp.int32, emb_ref.shape, 1) + lax.axis_index("tp") * first
    emb_ref[...] = time_embed(moment, channel)
    step_ref[...] = jnp.broadcast_to((b_ref[5:6, 0:size] - b_ref[4:5, 0:size]) / 1000.0, step_ref.shape)


def tables(stats, group_pos, first, count, size):
    four = jax.ShapeDtypeStruct((4, count, size), F32)
    two = jax.ShapeDtypeStruct((2, count, size), F32)
    return pl.pallas_call(
        functools.partial(tables_kernel, first),
        name="token_tables",
        in_specs=[pl.BlockSpec(memory_space=pltpu.SMEM)] + [VMEM] * 4,
        out_specs=[VMEM] * 8,
        out_shape=[four, four, four, four, two, two]
        + [jax.ShapeDtypeStruct((8, PERIOD), F32), jax.ShapeDtypeStruct((8, size), F32)],
        compiler_params=pltpu.CompilerParams(vmem_limit_bytes=LIMIT),
        cost_estimate=pl.CostEstimate(flops=count * size * 60, bytes_accessed=count * size * 80, transcendentals=0),
    )(group_pos, *stats)


def attend_kernel(
    heads, size,
    a_ref, near_ref, own_ref, far_ref, base_ref, amp_ref, q_ref, k_ref, v_ref,
    mean_ref, rstd_ref, ck_ref, sk_ref, cq_ref, sq_ref, emb_ref, step_ref, *rest,
):
    vel_ref, new_ref = rest[-2:]
    count = own_ref.shape[0]
    position = lax.axis_index("queue")
    odd = position % 2 == 1
    has_a, has_b, has_d = position > 1, position > 0, position < lax.axis_size("queue") - 1
    for h in range(heads):
        cut = slice(h * size, (h + 1) * size)
        start = pl.multiple_of((pl.program_id(0) * heads + h) * size, size)
        off = (h * size) % PERIOD
        near, far = near_ref[:, pl.ds(start, size)].astype(F32), far_ref[:, pl.ds(start, size)].astype(F32)
        x = [
            a_ref[:, pl.ds(start, size)].astype(F32),
            jnp.where(odd, near, far),
            own_ref[:, cut].astype(F32),
            jnp.where(odd, far, near),
        ]
        mod = lambda g, i: base_ref[i, :, cut] + amp_ref[i, :, cut] * emb_ref[g : g + 1, off : off + size]
        mixed = jnp.concatenate(
            [normed_mix(x[g], mean_ref[g], rstd_ref[g], mod(g, 0), mod(g, 1)) for g in range(4)], axis=0
        )
        both = jnp.concatenate([k_ref[h], v_ref[0, h]], axis=1)
        raw_kv = jnp.dot(mixed, both, preferred_element_type=F32)
        raw_q = jnp.dot(mixed[count : 3 * count], q_ref[h], preferred_element_type=F32)
        part = lambda raw, g: raw[g * count : (g + 1) * count]

        def turned(raw, cos, sin):
            return (raw * cos + pltpu.roll(raw, size // 2, 1) * sin).astype(BF16)

        key = [turned(part(raw_kv, g)[:, :size], ck_ref[g], sk_ref[g]) for g in range(4)]
        query = [turned(part(raw_q, g), cq_ref[g], sq_ref[g]) for g in range(2)]
        value = [part(raw_kv, g)[:, size:].astype(BF16) for g in range(4)]
        ones = [jnp.ones((count, size), BF16)] * 4
        for g, there in ((0, has_a), (1, has_b), (3, has_d)):
            key[g] = jnp.where(there, key[g], key[2])
            value[g] = jnp.where(there, value[g], jnp.zeros_like(value[g]))
            ones[g] = jnp.where(there, ones[g], jnp.zeros_like(ones[g]))
        outs = []
        for g in range(2):
            keys = jnp.concatenate(key[g : g + 3], axis=0)
            wide = jnp.concatenate(
                [jnp.concatenate(value[g : g + 3], axis=0), jnp.concatenate(ones[g : g + 3], axis=0)],
                axis=1,
            )
            scores = lax.dot_general(
                query[g], keys, (((1,), (1,)), ((), ())), preferred_element_type=F32
            )
            top = jnp.max(scores, axis=-1, keepdims=True)
            weights = jnp.exp2(scores - top).astype(BF16)
            total = jnp.dot(weights, wide, preferred_element_type=F32)
            outs.append(total[:, :size] / total[:, size:])
        state = x[2] + mod(2, 2) * outs[1]
        vel_ref[:, cut] = state.astype(BF16)
        state = x[1] + mod(1, 2) * outs[0]
        moved = x[1] + step_ref[0:1, :] * state
        new_ref[:, cut] = jnp.where(has_b, moved, 0.0).astype(BF16)


def attend(lo, hi, a, near, own, far, base, amp, q, k, v, tabs, sofar):
    count = own.shape[0]
    size = v.shape[2]
    heads = divisor(math.gcd(lo, hi - lo), STEP_HEADS)
    first = lo // heads
    whole = pl.BlockSpec((count, heads * size), lambda i: (0, i + first))
    modspec = pl.BlockSpec((base.shape[0], 1, heads * size), lambda i: (0, 0, i + first))
    single = pl.BlockSpec((heads, size, size), lambda i: (i + first, 0, 0))
    lone = pl.BlockSpec((1, heads, size, size), lambda i: (0, i + first, 0, 0))
    keys = 3 * count
    number = hi - lo
    ins = [VMEM, VMEM, whole, VMEM, modspec, modspec, single, single, lone] + [VMEM] * len(tabs)
    return pl.pallas_call(
        functools.partial(attend_kernel, heads, size),
        name="attend_heads",
        grid=(number // heads,),
        in_specs=ins + [pl.BlockSpec(memory_space=pl.ANY)] * len(sofar),
        out_specs=[whole] * 2,
        out_shape=[jax.ShapeDtypeStruct(own.shape, BF16)] * 2,
        input_output_aliases={len(ins) + i: i for i in range(len(sofar))},
        compiler_params=pltpu.CompilerParams(dimension_semantics=("arbitrary",), vmem_limit_bytes=LIMIT),
        cost_estimate=pl.CostEstimate(
            flops=number * (20 * count * size * size + 8 * count * keys * size),
            bytes_accessed=12 * count * number * size + 10 * number * size * size,
            transcendentals=2 * number * count * keys,
        ),
    )(a, near, own, far, base, amp, q, k, v, *tabs, *sofar)


def body(hidden, q_weight, k_weight, v_weight, mod_base, mod_amp, levels, steps_table, group_pos):
    count, local_width = hidden.shape
    local_heads, size = q_weight.shape[1], q_weight.shape[2]
    length = lax.axis_size("queue")
    width = local_width * lax.axis_size("tp")
    everyone = range(length)
    base = mod_base[0][:, None, :]
    amp = mod_amp[0][:, None, :]

    cuts = [2 * (local_heads // 2 * i // CHUNKS) for i in range(CHUNKS)] + [local_heads]
    *pieces, sums = split(hidden, cuts, size)
    near, back, far = [], [], []
    for piece in pieces:
        near.append(send(piece, [(i, i ^ 1) for i in everyone], length))
        back.append(send(piece, [(i, i + 2) for i in everyone], length))
    for piece in near:
        far.append(send(piece, [(i, i - 2 if i % 2 else i + 2) for i in everyone], length))

    peer = other_core(sums)
    squares = token_squares(hidden, sums, peer, levels, steps_table, base, amp, q_weight, k_weight, width)
    total = squares + other_core(squares)
    line = jnp.arange(8, dtype=jnp.int32)[:, None]
    factor = jnp.where(line == 2, math.log2(math.e) / math.sqrt(size), 1.0)
    own_stats = jnp.where((line == 2) | (line == 3), lax.rsqrt(total / width + 1e-06) * factor, squares)
    stats = [
        send(own_stats, [(i, i + 2) for i in everyone], length, wrap=True),
        send(own_stats, [(i, i + 1) for i in everyone], length, wrap=True),
        own_stats,
        send(own_stats, [(i, i - 1) for i in everyone], length, wrap=True),
    ]
    tabs = tables(stats, group_pos, local_width, count, size)
    apart = pairs_apart(size)
    q = jnp.einsum("hde,ef->hdf", q_weight[0], apart)
    k = jnp.einsum("hde,ef->hdf", k_weight[0], apart)

    outs = ()
    for c, (lo, hi) in enumerate(zip(cuts[:-1], cuts[1:])):
        outs = attend(lo, hi, back[c], near[c], hidden, far[c], base, amp, q, k, v_weight, tabs, outs)
    velocity, new_queue = outs
    return (new_queue, velocity)


def solution(mesh):
    return jax.shard_map(
        body,
        mesh=mesh,
        in_specs=(
            P(("groups", "queue"), "tp"),
            P(None, "tp", None, None),
            P(None, "tp", None, None),
            P(None, "tp", None, None),
            P(None, None, "tp"),
            P(None, None, "tp"),
            P(("groups", "queue")),
            P(),
            P("groups"),
        ),
        out_specs=(P(("groups", "queue"), "tp"), P(("groups", "queue"), "tp")),
        check_vma=False,
    )
```

```python
import functools
import math

import jax
import jax.numpy as jnp
from jax import lax
from jax.experimental import pallas as pl
from jax.experimental.pallas import tpu as pltpu
from jax.sharding import PartitionSpec as P

WIDE = 52
HW_DEV = 104
PERIOD = 256
CHUNKS = 2
SUM_HEADS = 5
LIMIT = 24 << 20
F32 = jnp.float32
BF16 = jnp.bfloat16
VMEM = pl.BlockSpec(memory_space=pltpu.VMEM)
HBM = pl.BlockSpec(memory_space=pltpu.HBM)


def send(array, pairs, length, wrap=False):
    if wrap:
        pairs = [(a, b % length) for a, b in pairs]
    pairs = [(a, b) for a, b in pairs if 0 <= b < length]
    return lax.ppermute(array, "queue", pairs)


def other_core(array):
    if lax.axis_size("tp") == 2:
        return lax.ppermute(array, "tp", [(0, 1), (1, 0)])
    return lax.psum(array, "tp") - array


def in_hbm(array):
    return pltpu.with_memory_space_constraint(array, pltpu.HBM)


def divisor(count, most):
    return max(k for k in range(1, most + 1) if count % k == 0)


def time_embed(moment, channel):
    within = channel % 256
    freq = jnp.exp(-jnp.log(10000.0) * (within % 128).astype(F32) / 128.0)
    angle = moment * freq
    return jnp.where(within < 128, jnp.cos(angle), jnp.sin(angle))


def pair_plan(shape, size):
    half = size // 2
    side = size // 6
    lead = (size - 4 * side) // 2
    pair = lax.broadcasted_iota(jnp.int32, shape, len(shape) - 1) % half
    part = jnp.where(pair < lead, 0, jnp.where(pair < lead + side, 1, 2))
    within = pair - jnp.where(part == 0, 0, jnp.where(part == 1, lead, lead + side))
    pairs = jnp.where(part == 0, lead, side).astype(F32)
    return part, jnp.exp(-math.log(10000.0) * (within.astype(F32) / pairs))


def block_maps(weight, apart):
    heads, size = weight.shape[:2]
    col = jnp.arange(2 * size)[None, :]
    half = size // 2
    if apart:
        source = 2 * (col % half) + col // size
        owner = col % size // half
    else:
        source = col % size
        owner = col // size
    spread = (jnp.arange(size)[:, None] == source).astype(BF16)
    full = jnp.einsum("pde,ef->pdf", weight.reshape(heads // 2, 2 * size, size), spread)
    mine = jnp.arange(2 * size)[:, None] // size == owner
    return jnp.where(mine, full, jnp.zeros_like(full))


def normed_mix(x, mean, rstd, shift, scale):
    return ((x - mean) * rstd * (1.0 + scale) + shift).astype(BF16)


def to_rows(columns, size):
    count = columns[0].shape[0]
    lane = lax.broadcasted_iota(jnp.int32, (count, size), 1)
    wide = jnp.zeros((count, size), F32)
    for j, column in enumerate(columns):
        wide = jnp.where(lane == j, jnp.broadcast_to(column, (count, size)), wide)
    return jnp.transpose(wide)[:8]


def split_kernel(size, cuts, x_hbm, *refs):
    outs, (x_ref, sums_ref, sems) = refs[: len(cuts) - 1], refs[len(cuts) - 1 :]
    count, _ = x_ref.shape
    blocks = []
    for piece, lo, hi in zip(outs, cuts[:-1], cuts[1:]):
        middle = (lo + hi) // 2
        for start, stop in ((lo, middle), (middle, hi)):
            here = slice(start * size, stop * size)
            there = slice((start - lo) * size, (stop - lo) * size)
            i = len(blocks)
            blocks.append(
                (
                    start,
                    stop,
                    pltpu.make_async_copy(x_hbm.at[:, here], x_ref.at[:, here], sems.at[0, i]),
                    pltpu.make_async_copy(x_ref.at[:, here], piece.at[:, there], sems.at[1, i]),
                )
            )
    for *_, come, _ in blocks:
        come.start()
    total = jnp.zeros((count, size), F32)
    second = jnp.zeros((count, size), F32)
    for start, stop, come, go in blocks:
        come.wait()
        go.start()
        for h in range(start, stop):
            x = x_ref[:, h * size : (h + 1) * size].astype(F32)
            total += x
            second += x * x
    sums_ref[...] = to_rows(
        [jnp.sum(total, axis=1, keepdims=True), jnp.sum(second, axis=1, keepdims=True)], size
    )
    for *_, go in blocks:
        go.wait()


def split(x, cuts, size):
    count, width = x.shape
    return pl.pallas_call(
        functools.partial(split_kernel, size, cuts),
        name="token_split",
        in_specs=[HBM],
        out_specs=[HBM] * (len(cuts) - 1) + [VMEM, VMEM],
        out_shape=[jax.ShapeDtypeStruct((count, (hi - lo) * size), BF16) for lo, hi in zip(cuts[:-1], cuts[1:])]
        + [jax.ShapeDtypeStruct(x.shape, BF16), jax.ShapeDtypeStruct((8, count), F32)],
        scratch_shapes=[pltpu.SemaphoreType.DMA((2, 2 * len(cuts) - 2))],
        compiler_params=pltpu.CompilerParams(vmem_limit_bytes=LIMIT),
        cost_estimate=pl.CostEstimate(flops=4 * count * width, bytes_accessed=4 * count * width, transcendentals=0),
    )(in_hbm(x))


def squares_kernel(
    width, level_ref, steps_hbm, x_ref, own_ref, peer_ref, base_hbm, amp_hbm, q_hbm, k_hbm,
    out_ref, acc, tab, emb, steps, base, amp, q_ref, k_ref, sems,
):
    count = x_ref.shape[0]
    local_heads, size = q_ref.shape[:2]
    share = divisor(local_heads, SUM_HEADS)
    small = [
        pltpu.make_async_copy(src, dst, sems.at[i])
        for i, (src, dst) in enumerate(((steps_hbm, steps), (base_hbm, base), (amp_hbm, amp)))
    ]
    large = [
        [
            pltpu.make_async_copy(
                src.at[0, lo : lo + share], dst.at[lo : lo + share], sems.at[3 + 2 * (lo // share) + i]
            )
            for i, (src, dst) in enumerate(((q_hbm, q_ref), (k_hbm, k_ref)))
        ]
        for lo in range(0, local_heads, share)
    ]
    for copy in small + sum(large, []):
        copy.start()
    acc[...] = jnp.zeros_like(acc)
    cols = jnp.transpose(own_ref[...] + peer_ref[...])
    mean = cols[:, 0:1] / width
    rstd = lax.rsqrt(cols[:, 1:2] / width - mean * mean + 1e-06)
    tab[0] = jnp.broadcast_to(mean, (count, size))
    tab[1] = jnp.broadcast_to(rstd, (count, size))
    for copy in small:
        copy.wait()
    moment = [steps[level_ref[0] + i].astype(F32) for i in range(2)]
    first = lax.axis_index("tp") * (width // lax.axis_size("tp"))
    emb[...] = time_embed(moment[0], lax.broadcasted_iota(jnp.int32, emb.shape, 1) + first)
    for h in range(local_heads):
        if h % share == 0:
            for copy in large[h // share]:
                copy.wait()
        cut = slice(h * size, (h + 1) * size)
        off = (h * size) % PERIOD
        mod = lambda i: base[i, :, cut] + amp[i, :, cut] * emb[0:1, off : off + size]
        mixed = normed_mix(x_ref[:, cut].astype(F32), tab[0], tab[1], mod(0), mod(1))
        both = jnp.concatenate([q_ref[h], k_ref[h]], axis=1)
        raw = jnp.dot(mixed, both, preferred_element_type=F32)
        acc[...] += raw * raw
    out_ref[...] = to_rows(
        [
            mean,
            rstd,
            jnp.sum(acc[:, :size], axis=1, keepdims=True),
            jnp.sum(acc[:, size:], axis=1, keepdims=True),
            jnp.full((count, 1), moment[0]),
            jnp.full((count, 1), moment[1]),
        ],
        size,
    )


def token_squares(x, own, peer, levels, steps_table, base, amp, q_weight, k_weight, width):
    count = x.shape[0]
    local_heads, size = q_weight.shape[1], q_weight.shape[2]
    number = local_heads // divisor(local_heads, SUM_HEADS)
    return pl.pallas_call(
        functools.partial(squares_kernel, width),
        name="token_squares",
        in_specs=[pl.BlockSpec(memory_space=pltpu.SMEM), HBM, VMEM, VMEM, VMEM] + [HBM] * 4,
        out_specs=VMEM,
        out_shape=jax.ShapeDtypeStruct((8, count), F32),
        scratch_shapes=[
            pltpu.VMEM((count, 2 * size), F32),
            pltpu.VMEM((2, count, size), F32),
            pltpu.VMEM((8, PERIOD), F32),
            pltpu.SMEM(steps_table.shape, jnp.int32),
            pltpu.VMEM(base.shape, F32),
            pltpu.VMEM(amp.shape, F32),
            pltpu.VMEM(q_weight.shape[1:], BF16),
            pltpu.VMEM(k_weight.shape[1:], BF16),
            pltpu.SemaphoreType.DMA((3 + 2 * number,)),
        ],
        compiler_params=pltpu.CompilerParams(vmem_limit_bytes=LIMIT),
        cost_estimate=pl.CostEstimate(
            flops=4 * count * local_heads * size * size,
            bytes_accessed=2 * count * local_heads * size + 4 * local_heads * size * size,
            transcendentals=0,
        ),
    )(levels, in_hbm(steps_table), x, own, peer, *map(in_hbm, (base, amp, q_weight, k_weight)))


def tables_kernel(
    first, pos_ref, a_ref, b_ref, c_ref, d_ref,
    mean_ref, rstd_ref, ck_ref, sk_ref, cq_ref, sq_ref, emb_ref, step_ref,
):
    count, size = mean_ref.shape[1:]
    frames = -(-count // HW_DEV)
    position = lax.axis_index("queue")
    last = lax.axis_size("queue") - 1
    inner = lax.broadcasted_iota(jnp.int32, (HW_DEV, size), 0)
    part, freq = pair_plan((HW_DEV, size), size)
    hpos = (inner // WIDE).astype(F32)
    wpos = (inner % WIDE).astype(F32)
    angle = jnp.where(part == 1, hpos, wpos) * freq
    pcos, psin = jnp.cos(angle), jnp.sin(angle)
    row = lax.broadcasted_iota(jnp.int32, (8, size), 0)
    _, ffreq = pair_plan((8, size), size)
    emb_row = lax.broadcasted_iota(jnp.int32, emb_ref.shape, 0)
    moment = jnp.zeros(emb_ref.shape, F32)
    for g, stats in enumerate((a_ref, b_ref, c_ref, d_ref)):
        start = pos_ref[jnp.clip(position + (g - 2), 0, last)]
        fangle = (start + row).astype(F32) * ffreq
        fcos, fsin = jnp.cos(fangle), jnp.sin(fangle)
        cols = jnp.transpose(stats[...])
        moment = jnp.where(emb_row == g, stats[4:5, 0:1], moment)
        for f in range(frames):
            lo, hi = f * HW_DEV, min((f + 1) * HW_DEV, count)
            cos = jnp.where(part == 0, fcos[f : f + 1], pcos)[: hi - lo]
            sin = jnp.where(part == 0, fsin[f : f + 1], psin)[: hi - lo]
            column = lambda j: jnp.broadcast_to(cols[lo:hi, j : j + 1], (hi - lo, size))
            mean_ref[g, lo:hi] = column(0)
            rstd_ref[g, lo:hi] = column(1)
            ck_ref[g, lo:hi] = cos * column(3)
            sk_ref[g, lo:hi] = sin * column(3)
            if g in (1, 2):
                cq_ref[g - 1, lo:hi] = cos * column(2)
                sq_ref[g - 1, lo:hi] = sin * column(2)
    channel = lax.broadcasted_iota(jnp.int32, emb_ref.shape, 1) + lax.axis_index("tp") * first
    emb_ref[...] = time_embed(moment, channel)
    step_ref[...] = jnp.broadcast_to((b_ref[5:6, 0:size] - b_ref[4:5, 0:size]) / 1000.0, step_ref.shape)


def tables(stats, group_pos, first, count, size):
    four = jax.ShapeDtypeStruct((4, count, size), F32)
    two = jax.ShapeDtypeStruct((2, count, size), F32)
    return pl.pallas_call(
        functools.partial(tables_kernel, first),
        name="token_tables",
        in_specs=[pl.BlockSpec(memory_space=pltpu.SMEM)] + [VMEM] * 4,
        out_specs=[VMEM] * 8,
        out_shape=[four, four, four, four, two, two]
        + [jax.ShapeDtypeStruct((8, PERIOD), F32), jax.ShapeDtypeStruct((8, size), F32)],
        compiler_params=pltpu.CompilerParams(vmem_limit_bytes=LIMIT),
        cost_estimate=pl.CostEstimate(flops=count * size * 60, bytes_accessed=count * size * 80, transcendentals=0),
    )(group_pos, *stats)


def attend_kernel(
    lo, number, size, relayed,
    near_ref, own_ref, ahead_ref, across_ref, base_ref, amp_ref, q_ref, k_ref, v_ref,
    mean_ref, rstd_ref, ck_ref, sk_ref, cq_ref, sq_ref, emb_ref, step_ref, *rest,
):
    vel_hbm, new_hbm, keys, wide, queries, vel_out, new_out, sems = rest[-8:]
    count = own_ref.shape[0]
    two = 2 * size
    first = lo // 2
    position = lax.axis_index("queue")
    odd = position % 2 == 1
    has_b = position > 0
    there = {0: position > 1, 1: has_b, 3: position < lax.axis_size("queue") - 1}
    rows = lambda g: slice(g * count, (g + 1) * count)
    half = (slice(0, size), slice(size, two))

    def lanes(pair, side):
        return pl.ds(pl.multiple_of(pair * two + side * size, size), size)

    def tokens(pair, side, g):
        held = lambda ref: ref[:, lanes(pair, side)]
        if g == 2:
            return own_ref[:, lanes(first + pair, side)].astype(F32)
        if g == 0:
            back = held(ahead_ref)
            if relayed:
                back = jnp.where(odd, back, held(rest[0]))
            return back.astype(F32)
        near, far = held(near_ref), held(across_ref)
        if relayed:
            far = jnp.where(odd, far, held(rest[1]))
        return (jnp.where(odd, near, far) if g == 1 else jnp.where(odd, far, near)).astype(F32)

    def mod(pair, side, g, i):
        off = (side * size) % PERIOD
        cut = lanes(first + pair, side)
        return base_ref[i, :, cut] + amp_ref[i, :, cut] * emb_ref[g : g + 1, off : off + size]

    def mix(pair, g):
        return jnp.concatenate(
            [
                normed_mix(
                    tokens(pair, side, g), mean_ref[g], rstd_ref[g], mod(pair, side, g, 0), mod(pair, side, g, 1)
                )
                for side in range(2)
            ],
            axis=1,
        )

    def turned(raw, cos, sin):
        one, other = raw[:, :size], raw[:, size:]
        return (one * cos - other * sin).astype(BF16), (one * sin + other * cos).astype(BF16)

    def project(pair, slot, g, mixed):
        key = turned(jnp.dot(mixed, k_ref[first + pair], preferred_element_type=F32), ck_ref[g], sk_ref[g])
        raw = jnp.dot(mixed, v_ref[first + pair], preferred_element_type=F32).astype(BF16)
        for i in range(2):
            value = raw[:, half[i]]
            part = key[i]
            if g in there:
                part = jnp.where(there[g], part, keys[slot, rows(2), half[i]])
                value = jnp.where(there[g], value, jnp.zeros_like(value))
            keys[slot, rows(g), half[i]] = part
            wide[slot, i, rows(g), :size] = value
        if g in (1, 2):
            raw = jnp.dot(mixed, q_ref[first + pair], preferred_element_type=F32)
            parts = turned(raw, cq_ref[g - 1], sq_ref[g - 1])
            lane = lax.broadcasted_iota(jnp.int32, (1, size), 1)
            for side in range(2):
                mine = (lane < size // 2) == (side == 0)
                for i in range(2):
                    queries[slot, g - 1, rows(side), half[i]] = jnp.where(mine, parts[i], jnp.zeros_like(parts[i]))

    def score(slot, g):
        return lax.dot_general(
            queries[slot, g],
            keys[slot, g * count : (g + 3) * count],
            (((1,), (1,)), ((), ())),
            preferred_element_type=F32,
        )

    def soften(scores):
        top = jnp.max(scores, axis=-1, keepdims=True)
        return jnp.exp2(scores - top).astype(BF16)

    def gather(slot, side, g, weights):
        total = jnp.dot(weights, wide[slot, side, g * count : (g + 3) * count], preferred_element_type=F32)
        return total[:, :size] / total[:, size:]

    def finish(pair, slot, side, g, attn):
        x = tokens(pair, side, g + 1)
        state = x + mod(pair, side, g + 1, 2) * attn
        if g == 1:
            vel_out[slot, :, half[side]] = state.astype(BF16)
        else:
            moved = x + step_ref[0:1, :] * state
            new_out[slot, :, half[side]] = jnp.where(has_b, moved, 0.0).astype(BF16)

    def copies(pair, slot):
        to = pl.ds(pl.multiple_of((first + pair) * two, two), two)
        return [
            pltpu.make_async_copy(out.at[slot], hbm.at[:, to], sems.at[i, slot])
            for i, (out, hbm) in enumerate(((vel_out, vel_hbm), (new_out, new_hbm)))
        ]

    def attention(pair, slot, following):
        other = 1 - slot
        if isinstance(pair, int):
            if pair >= 2:
                for copy in copies(pair - 2, slot):
                    copy.wait()
        else:
            @pl.when(pair >= 2)
            def _():
                for copy in copies(pair - 2, slot):
                    copy.wait()

        for g, groups in ((0, (2, 1)), (1, (0, 3))):
            scores = score(slot, g)
            if following:
                mixed = [mix(pair + 1, j) for j in groups]
            weights = soften(scores[rows(0)])
            if following:
                project(pair + 1, other, groups[0], mixed[0])
            total = gather(slot, 0, g, weights)
            weights = soften(scores[rows(1)])
            finish(pair, slot, 0, g, total)
            if following:
                project(pair + 1, other, groups[1], mixed[1])
            total = gather(slot, 1, g, weights)
            finish(pair, slot, 1, g, total)
        for copy in copies(pair, slot):
            copy.start()

    pairs = number // 2
    for g in range(4):
        ones = jnp.ones((count, size), BF16)
        if g in there:
            ones = jnp.where(there[g], ones, jnp.zeros_like(ones))
        for slot in range(2):
            for side in range(2):
                wide[slot, side, rows(g), size:] = ones
    for g in (2, 1, 0, 3):
        project(0, 0, g, mix(0, g))
    looped = (pairs - 1) // 2

    def step(i, _):
        attention(2 * i, 0, True)
        attention(2 * i + 1, 1, True)

    lax.fori_loop(0, looped, step, None)
    for pair in range(2 * looped, pairs):
        attention(pair, pair % 2, pair < pairs - 1)
    for pair in range(max(0, pairs - 2), pairs):
        for copy in copies(pair, pair % 2):
            copy.wait()


def attend(lo, hi, near, own, ahead, across, relay, base, amp, q, k, v, tabs, sofar):
    count = own.shape[0]
    size = v.shape[2] // 2
    keys = 3 * count
    number = hi - lo
    hbm = pl.BlockSpec(memory_space=pl.ANY)
    ins = [VMEM] * (9 + len(tabs) + len(relay))
    return pl.pallas_call(
        functools.partial(attend_kernel, lo, number, size, bool(relay)),
        name="attend_heads",
        in_specs=ins + [hbm] * len(sofar),
        out_specs=[hbm] * 2,
        out_shape=[jax.ShapeDtypeStruct(own.shape, BF16)] * 2,
        scratch_shapes=[
            pltpu.VMEM((2, 4 * count, 2 * size), BF16),
            pltpu.VMEM((2, 2, 4 * count, 2 * size), BF16),
            pltpu.VMEM((2, 2, 2 * count, 2 * size), BF16),
            pltpu.VMEM((2, count, 2 * size), BF16),
            pltpu.VMEM((2, count, 2 * size), BF16),
            pltpu.SemaphoreType.DMA((2, 2)),
        ],
        input_output_aliases={len(ins) + i: i for i in range(len(sofar))},
        compiler_params=pltpu.CompilerParams(vmem_limit_bytes=LIMIT),
        cost_estimate=pl.CostEstimate(
            flops=number * (20 * count * size * size + 8 * count * keys * size),
            bytes_accessed=12 * count * number * size + 10 * number * size * size,
            transcendentals=2 * number * count * keys,
        ),
    )(near, own, ahead, across, base, amp, q, k, v, *tabs, *relay, *sofar)


def body(hidden, q_weight, k_weight, v_weight, mod_base, mod_amp, levels, steps_table, group_pos):
    count, local_width = hidden.shape
    local_heads, size = q_weight.shape[1], q_weight.shape[2]
    length = lax.axis_size("queue")
    width = local_width * lax.axis_size("tp")
    everyone = range(length)
    base = mod_base[0][:, None, :]
    amp = mod_amp[0][:, None, :]

    cuts = [2 * (local_heads // 2 * i // CHUNKS) for i in range(CHUNKS)] + [local_heads]
    *pieces, rows, sums = split(hidden, cuts, size)
    swap = [(i, i ^ 1) for i in everyone]
    two_on = [(i, i + 2) for i in everyone]
    both_ways = [(i, i - 2 if i % 2 else i + 2) for i in everyone]
    near, ahead, across, more = [], [], [], []
    for c, piece in enumerate(pieces):
        near.append(send(piece, swap, length))
        if c < CHUNKS - 1 or length % 2:
            ahead.append(send(piece, two_on, length))
            across.append(send(near[c], both_ways, length))
            more.append(())
        else:
            ahead.append(send(piece, two_on[1::2], length))
            across.append(send(near[c], both_ways[1::2], length))
            even = send(piece, two_on[0::2], length)
            more.append((even, send(ahead[c], swap, length)))

    peer = other_core(sums)
    squares = token_squares(rows, sums, peer, levels, steps_table, base, amp, q_weight, k_weight, width)
    total = squares + other_core(squares)
    line = jnp.arange(8, dtype=jnp.int32)[:, None]
    factor = jnp.where(line == 2, math.log2(math.e) / math.sqrt(size), 1.0)
    own_stats = jnp.where((line == 2) | (line == 3), lax.rsqrt(total / width + 1e-06) * factor, squares)
    stats = [
        send(own_stats, [(i, i + 2) for i in everyone], length, wrap=True),
        send(own_stats, [(i, i + 1) for i in everyone], length, wrap=True),
        own_stats,
        send(own_stats, [(i, i - 1) for i in everyone], length, wrap=True),
    ]
    tabs = tables(stats, group_pos, local_width, count, size)
    q = block_maps(q_weight[0], True)
    k = block_maps(k_weight[0], True)
    v = block_maps(v_weight[0], False)

    outs = ()
    for c, (lo, hi) in enumerate(zip(cuts[:-1], cuts[1:])):
        outs = attend(lo, hi, near[c], rows, ahead[c], across[c], more[c], base, amp, q, k, v, tabs, outs)
    velocity, new_queue = outs
    return (new_queue, velocity)


def solution(mesh):
    return jax.shard_map(
        body,
        mesh=mesh,
        in_specs=(
            P(("groups", "queue"), "tp"),
            P(None, "tp", None, None),
            P(None, "tp", None, None),
            P(None, "tp", None, None),
            P(None, None, "tp"),
            P(None, None, "tp"),
            P(("groups", "queue")),
            P(),
            P("groups"),
        ),
        out_specs=(P(("groups", "queue"), "tp"), P(("groups", "queue"), "tp")),
        check_vma=False,
    )
```

```python
import functools
import math

import jax
import jax.numpy as jnp
from jax import lax
from jax.experimental import pallas as pl
from jax.experimental.pallas import tpu as pltpu
from jax.sharding import PartitionSpec as P

WIDE = 52
HW_DEV = 104
PERIOD = 256
CHUNKS = 2
FIRST = 0.5
SUM_HEADS = 5
LIMIT = 24 << 20
F32 = jnp.float32
BF16 = jnp.bfloat16
VMEM = pl.BlockSpec(memory_space=pltpu.VMEM)
HBM = pl.BlockSpec(memory_space=pltpu.HBM)


def send(array, pairs, length, wrap=False):
    if wrap:
        pairs = [(a, b % length) for a, b in pairs]
    pairs = [(a, b) for a, b in pairs if 0 <= b < length]
    return lax.ppermute(array, "queue", pairs)


def other_core(array):
    if lax.axis_size("tp") == 2:
        return lax.ppermute(array, "tp", [(0, 1), (1, 0)])
    return lax.psum(array, "tp") - array


def in_hbm(array):
    return pltpu.with_memory_space_constraint(array, pltpu.HBM)


def divisor(count, most):
    return max(k for k in range(1, most + 1) if count % k == 0)


def time_embed(moment, channel):
    within = channel % 256
    freq = jnp.exp(-jnp.log(10000.0) * (within % 128).astype(F32) / 128.0)
    angle = moment * freq
    return jnp.where(within < 128, jnp.cos(angle), jnp.sin(angle))


def pair_plan(shape, size):
    half = size // 2
    side = size // 6
    lead = (size - 4 * side) // 2
    pair = lax.broadcasted_iota(jnp.int32, shape, len(shape) - 1) % half
    part = jnp.where(pair < lead, 0, jnp.where(pair < lead + side, 1, 2))
    within = pair - jnp.where(part == 0, 0, jnp.where(part == 1, lead, lead + side))
    pairs = jnp.where(part == 0, lead, side).astype(F32)
    return part, jnp.exp(-math.log(10000.0) * (within.astype(F32) / pairs))


def block_maps(weight, apart):
    heads, size = weight.shape[:2]
    col = jnp.arange(2 * size)[None, :]
    half = size // 2
    if apart:
        source = 2 * (col % half) + col // size
        owner = col % size // half
    else:
        source = col % size
        owner = col // size
    spread = (jnp.arange(size)[:, None] == source).astype(BF16)
    full = jnp.einsum("pde,ef->pdf", weight.reshape(heads // 2, 2 * size, size), spread)
    mine = jnp.arange(2 * size)[:, None] // size == owner
    return jnp.where(mine, full, jnp.zeros_like(full))


def normed_mix(x, mean, rstd, shift, scale):
    return ((x - mean) * rstd * (1.0 + scale) + shift).astype(BF16)


def to_rows(columns, size):
    count = columns[0].shape[0]
    lane = lax.broadcasted_iota(jnp.int32, (count, size), 1)
    wide = jnp.zeros((count, size), F32)
    for j, column in enumerate(columns):
        wide = jnp.where(lane == j, jnp.broadcast_to(column, (count, size)), wide)
    return jnp.transpose(wide)[:8]


def split_kernel(size, cuts, x_hbm, *refs):
    outs, (x_ref, sums_ref, sems) = refs[: len(cuts) - 1], refs[len(cuts) - 1 :]
    count, _ = x_ref.shape
    blocks = []
    for piece, lo, hi in zip(outs, cuts[:-1], cuts[1:]):
        middle = (lo + hi) // 2
        for start, stop in ((lo, middle), (middle, hi)):
            here = slice(start * size, stop * size)
            there = slice((start - lo) * size, (stop - lo) * size)
            i = len(blocks)
            blocks.append(
                (
                    start,
                    stop,
                    pltpu.make_async_copy(x_hbm.at[:, here], x_ref.at[:, here], sems.at[0, i]),
                    pltpu.make_async_copy(x_ref.at[:, here], piece.at[:, there], sems.at[1, i]),
                )
            )
    for *_, come, _ in blocks:
        come.start()
    total = jnp.zeros((count, size), F32)
    second = jnp.zeros((count, size), F32)
    for start, stop, come, go in blocks:
        come.wait()
        go.start()
        for h in range(start, stop):
            x = x_ref[:, h * size : (h + 1) * size].astype(F32)
            total += x
            second += x * x
    sums_ref[...] = to_rows(
        [jnp.sum(total, axis=1, keepdims=True), jnp.sum(second, axis=1, keepdims=True)], size
    )
    for *_, go in blocks:
        go.wait()


def split(x, cuts, size):
    count, width = x.shape
    return pl.pallas_call(
        functools.partial(split_kernel, size, cuts),
        name="token_split",
        in_specs=[HBM],
        out_specs=[HBM] * (len(cuts) - 1) + [VMEM, VMEM],
        out_shape=[jax.ShapeDtypeStruct((count, (hi - lo) * size), BF16) for lo, hi in zip(cuts[:-1], cuts[1:])]
        + [jax.ShapeDtypeStruct(x.shape, BF16), jax.ShapeDtypeStruct((8, count), F32)],
        scratch_shapes=[pltpu.SemaphoreType.DMA((2, 2 * len(cuts) - 2))],
        compiler_params=pltpu.CompilerParams(vmem_limit_bytes=LIMIT),
        cost_estimate=pl.CostEstimate(flops=4 * count * width, bytes_accessed=4 * count * width, transcendentals=0),
    )(in_hbm(x))


def squares_kernel(
    width, level_ref, steps_hbm, x_ref, own_ref, peer_ref, base_hbm, amp_hbm, q_hbm, k_hbm,
    out_ref, acc, tab, emb, steps, base, amp, q_ref, k_ref, sems,
):
    count = x_ref.shape[0]
    local_heads, size = q_ref.shape[:2]
    share = divisor(local_heads, SUM_HEADS)
    small = [
        pltpu.make_async_copy(src, dst, sems.at[i])
        for i, (src, dst) in enumerate(((steps_hbm, steps), (base_hbm, base), (amp_hbm, amp)))
    ]
    large = [
        [
            pltpu.make_async_copy(
                src.at[0, lo : lo + share], dst.at[lo : lo + share], sems.at[3 + 2 * (lo // share) + i]
            )
            for i, (src, dst) in enumerate(((q_hbm, q_ref), (k_hbm, k_ref)))
        ]
        for lo in range(0, local_heads, share)
    ]
    for copy in small + sum(large, []):
        copy.start()
    acc[...] = jnp.zeros_like(acc)
    cols = jnp.transpose(own_ref[...] + peer_ref[...])
    mean = cols[:, 0:1] / width
    rstd = lax.rsqrt(cols[:, 1:2] / width - mean * mean + 1e-06)
    tab[0] = jnp.broadcast_to(mean, (count, size))
    tab[1] = jnp.broadcast_to(rstd, (count, size))
    for copy in small:
        copy.wait()
    moment = [steps[level_ref[0] + i].astype(F32) for i in range(2)]
    first = lax.axis_index("tp") * (width // lax.axis_size("tp"))
    emb[...] = time_embed(moment[0], lax.broadcasted_iota(jnp.int32, emb.shape, 1) + first)
    for h in range(local_heads):
        if h % share == 0:
            for copy in large[h // share]:
                copy.wait()
        cut = slice(h * size, (h + 1) * size)
        off = (h * size) % PERIOD
        mod = lambda i: base[i, :, cut] + amp[i, :, cut] * emb[0:1, off : off + size]
        mixed = normed_mix(x_ref[:, cut].astype(F32), tab[0], tab[1], mod(0), mod(1))
        both = jnp.concatenate([q_ref[h], k_ref[h]], axis=1)
        raw = jnp.dot(mixed, both, preferred_element_type=F32)
        acc[...] += raw * raw
    out_ref[...] = to_rows(
        [
            mean,
            rstd,
            jnp.sum(acc[:, :size], axis=1, keepdims=True),
            jnp.sum(acc[:, size:], axis=1, keepdims=True),
            jnp.full((count, 1), moment[0]),
            jnp.full((count, 1), moment[1]),
        ],
        size,
    )


def token_squares(x, own, peer, levels, steps_table, base, amp, q_weight, k_weight, width):
    count = x.shape[0]
    local_heads, size = q_weight.shape[1], q_weight.shape[2]
    number = local_heads // divisor(local_heads, SUM_HEADS)
    return pl.pallas_call(
        functools.partial(squares_kernel, width),
        name="token_squares",
        in_specs=[pl.BlockSpec(memory_space=pltpu.SMEM), HBM, VMEM, VMEM, VMEM] + [HBM] * 4,
        out_specs=VMEM,
        out_shape=jax.ShapeDtypeStruct((8, count), F32),
        scratch_shapes=[
            pltpu.VMEM((count, 2 * size), F32),
            pltpu.VMEM((2, count, size), F32),
            pltpu.VMEM((8, PERIOD), F32),
            pltpu.SMEM(steps_table.shape, jnp.int32),
            pltpu.VMEM(base.shape, F32),
            pltpu.VMEM(amp.shape, F32),
            pltpu.VMEM(q_weight.shape[1:], BF16),
            pltpu.VMEM(k_weight.shape[1:], BF16),
            pltpu.SemaphoreType.DMA((3 + 2 * number,)),
        ],
        compiler_params=pltpu.CompilerParams(vmem_limit_bytes=LIMIT),
        cost_estimate=pl.CostEstimate(
            flops=4 * count * local_heads * size * size,
            bytes_accessed=2 * count * local_heads * size + 4 * local_heads * size * size,
            transcendentals=0,
        ),
    )(levels, in_hbm(steps_table), x, own, peer, *map(in_hbm, (base, amp, q_weight, k_weight)))


def tables_kernel(
    first, pos_ref, a_ref, b_ref, c_ref, d_ref,
    mean_ref, rstd_ref, ck_ref, sk_ref, cq_ref, sq_ref, emb_ref, step_ref,
):
    count, size = mean_ref.shape[1:]
    frames = -(-count // HW_DEV)
    position = lax.axis_index("queue")
    last = lax.axis_size("queue") - 1
    inner = lax.broadcasted_iota(jnp.int32, (HW_DEV, size), 0)
    part, freq = pair_plan((HW_DEV, size), size)
    hpos = (inner // WIDE).astype(F32)
    wpos = (inner % WIDE).astype(F32)
    angle = jnp.where(part == 1, hpos, wpos) * freq
    pcos, psin = jnp.cos(angle), jnp.sin(angle)
    row = lax.broadcasted_iota(jnp.int32, (8, size), 0)
    _, ffreq = pair_plan((8, size), size)
    emb_row = lax.broadcasted_iota(jnp.int32, emb_ref.shape, 0)
    moment = jnp.zeros(emb_ref.shape, F32)
    for g, stats in enumerate((a_ref, b_ref, c_ref, d_ref)):
        start = pos_ref[jnp.clip(position + (g - 2), 0, last)]
        fangle = (start + row).astype(F32) * ffreq
        fcos, fsin = jnp.cos(fangle), jnp.sin(fangle)
        cols = jnp.transpose(stats[...])
        moment = jnp.where(emb_row == g, stats[4:5, 0:1], moment)
        for f in range(frames):
            lo, hi = f * HW_DEV, min((f + 1) * HW_DEV, count)
            cos = jnp.where(part == 0, fcos[f : f + 1], pcos)[: hi - lo]
            sin = jnp.where(part == 0, fsin[f : f + 1], psin)[: hi - lo]
            column = lambda j: jnp.broadcast_to(cols[lo:hi, j : j + 1], (hi - lo, size))
            mean_ref[g, lo:hi] = column(0)
            rstd_ref[g, lo:hi] = column(1)
            ck_ref[g, lo:hi] = cos * column(3)
            sk_ref[g, lo:hi] = sin * column(3)
            if g in (1, 2):
                cq_ref[g - 1, lo:hi] = cos * column(2)
                sq_ref[g - 1, lo:hi] = sin * column(2)
    channel = lax.broadcasted_iota(jnp.int32, emb_ref.shape, 1) + lax.axis_index("tp") * first
    emb_ref[...] = time_embed(moment, channel)
    step_ref[...] = jnp.broadcast_to((b_ref[5:6, 0:size] - b_ref[4:5, 0:size]) / 1000.0, step_ref.shape)


def tables(stats, group_pos, first, count, size):
    four = jax.ShapeDtypeStruct((4, count, size), F32)
    two = jax.ShapeDtypeStruct((2, count, size), F32)
    return pl.pallas_call(
        functools.partial(tables_kernel, first),
        name="token_tables",
        in_specs=[pl.BlockSpec(memory_space=pltpu.SMEM)] + [VMEM] * 4,
        out_specs=[VMEM] * 8,
        out_shape=[four, four, four, four, two, two]
        + [jax.ShapeDtypeStruct((8, PERIOD), F32), jax.ShapeDtypeStruct((8, size), F32)],
        compiler_params=pltpu.CompilerParams(vmem_limit_bytes=LIMIT),
        cost_estimate=pl.CostEstimate(flops=count * size * 60, bytes_accessed=count * size * 80, transcendentals=0),
    )(group_pos, *stats)


def attend_kernel(
    lo, number, size, relayed,
    near_ref, own_ref, ahead_ref, across_ref, base_ref, amp_ref, q_ref, k_ref, v_ref,
    mean_ref, rstd_ref, ck_ref, sk_ref, cq_ref, sq_ref, emb_ref, step_ref, *rest,
):
    vel_hbm, new_hbm, keys, values, counted, queries, vel_out, new_out, sems = rest[-9:]
    count = own_ref.shape[0]
    two = 2 * size
    first = lo // 2
    position = lax.axis_index("queue")
    odd = position % 2 == 1
    has_b = position > 0
    there = {0: position > 1, 1: has_b, 3: position < lax.axis_size("queue") - 1}
    rows = lambda g: slice(g * count, (g + 1) * count)
    half = (slice(0, size), slice(size, two))

    def lanes(pair, side):
        return pl.ds(pl.multiple_of(pair * two + side * size, size), size)

    def tokens(pair, side, g):
        held = lambda ref: ref[:, lanes(pair, side)]
        if g == 2:
            return own_ref[:, lanes(first + pair, side)].astype(F32)
        if g == 0:
            back = held(ahead_ref)
            if relayed:
                back = jnp.where(odd, back, held(rest[0]))
            return back.astype(F32)
        near, far = held(near_ref), held(across_ref)
        if relayed:
            far = jnp.where(odd, far, held(rest[1]))
        return (jnp.where(odd, near, far) if g == 1 else jnp.where(odd, far, near)).astype(F32)

    def mod(pair, side, g, i):
        off = (side * size) % PERIOD
        cut = lanes(first + pair, side)
        return base_ref[i, :, cut] + amp_ref[i, :, cut] * emb_ref[g : g + 1, off : off + size]

    def mix(pair, g):
        return jnp.concatenate(
            [
                normed_mix(
                    tokens(pair, side, g), mean_ref[g], rstd_ref[g], mod(pair, side, g, 0), mod(pair, side, g, 1)
                )
                for side in range(2)
            ],
            axis=1,
        )

    def turned(raw, cos, sin):
        one, other = raw[:, :size], raw[:, size:]
        return (one * cos - other * sin).astype(BF16), (one * sin + other * cos).astype(BF16)

    def project(pair, slot, g, mixed):
        key = turned(jnp.dot(mixed, k_ref[first + pair], preferred_element_type=F32), ck_ref[g], sk_ref[g])
        raw = jnp.dot(mixed, v_ref[first + pair], preferred_element_type=F32).astype(BF16)
        for i in range(2):
            value = raw[:, half[i]]
            part = key[i]
            if g in there:
                part = jnp.where(there[g], part, keys[slot, i, rows(2)])
                value = jnp.where(there[g], value, jnp.zeros_like(value))
            keys[slot, i, rows(g)] = part
            values[slot, i, rows(g)] = value
        if g in (1, 2):
            raw = jnp.dot(mixed, q_ref[first + pair], preferred_element_type=F32)
            parts = turned(raw, cq_ref[g - 1], sq_ref[g - 1])
            lane = lax.broadcasted_iota(jnp.int32, (1, size), 1)
            for side in range(2):
                mine = (lane < size // 2) == (side == 0)
                for i in range(2):
                    queries[slot, i, rows(2 * (g - 1) + side)] = jnp.where(mine, parts[i], jnp.zeros_like(parts[i]))

    def dot_keys(slot, query_rows, span):
        return lax.dot_general(
            jnp.concatenate([queries[slot, i, query_rows] for i in range(2)], axis=1),
            jnp.concatenate([keys[slot, i, span] for i in range(2)], axis=1),
            (((1,), (1,)), ((), ())),
            preferred_element_type=F32,
        )

    def soften(shared, single):
        top = jnp.maximum(jnp.max(shared, axis=-1, keepdims=True), jnp.max(single, axis=-1, keepdims=True))
        return jnp.exp2(shared - top).astype(BF16), jnp.exp2(single - top).astype(BF16)

    def gather(slot, side, weights):
        wide = lambda span: jnp.concatenate([values[slot, side, span], counted[span]], axis=1)
        common = slice(count, 3 * count)
        total = jnp.dot(
            jnp.concatenate([shared for shared, _ in weights], axis=0), wide(common), preferred_element_type=F32
        )
        outs = []
        for g, own in ((0, 0), (1, 3)):
            part = total[rows(g)] + jnp.dot(weights[g][1], wide(rows(own)), preferred_element_type=F32)
            outs.append(part[:, :size] / part[:, size:])
        return outs

    def finish(pair, slot, side, g, attn):
        x = tokens(pair, side, g + 1)
        state = x + mod(pair, side, g + 1, 2) * attn
        if g == 1:
            vel_out[slot, :, half[side]] = state.astype(BF16)
        else:
            moved = x + step_ref[0:1, :] * state
            new_out[slot, :, half[side]] = jnp.where(has_b, moved, 0.0).astype(BF16)

    def copies(pair, slot):
        to = pl.ds(pl.multiple_of((first + pair) * two, two), two)
        return [
            pltpu.make_async_copy(out.at[slot], hbm.at[:, to], sems.at[i, slot])
            for i, (out, hbm) in enumerate(((vel_out, vel_hbm), (new_out, new_hbm)))
        ]

    def attention(pair, slot, following):
        other = 1 - slot
        if isinstance(pair, int):
            if pair >= 2:
                for copy in copies(pair - 2, slot):
                    copy.wait()
        else:
            @pl.when(pair >= 2)
            def _():
                for copy in copies(pair - 2, slot):
                    copy.wait()

        shared = dot_keys(slot, slice(0, 4 * count), slice(count, 3 * count))
        single = [
            dot_keys(slot, slice(0, 2 * count), rows(0)),
            dot_keys(slot, slice(2 * count, 4 * count), rows(3)),
        ]
        for side, groups in ((0, (2, 1)), (1, (0, 3))):
            if following:
                mixed = [mix(pair + 1, j) for j in groups]
            weights = [soften(shared[rows(2 * g + side)], single[g][rows(side)]) for g in range(2)]
            if following:
                for j, m in zip(groups, mixed):
                    project(pair + 1, other, j, m)
            for g, total in enumerate(gather(slot, side, weights)):
                finish(pair, slot, side, g, total)
        for copy in copies(pair, slot):
            copy.start()

    pairs = number // 2
    for g in range(4):
        ones = jnp.ones((count, size), BF16)
        if g in there:
            ones = jnp.where(there[g], ones, jnp.zeros_like(ones))
        counted[rows(g)] = ones
    for g in (2, 1, 0, 3):
        project(0, 0, g, mix(0, g))
    looped = (pairs - 1) // 2

    def step(i, _):
        attention(2 * i, 0, True)
        attention(2 * i + 1, 1, True)

    lax.fori_loop(0, looped, step, None)
    for pair in range(2 * looped, pairs):
        attention(pair, pair % 2, pair < pairs - 1)
    for pair in range(max(0, pairs - 2), pairs):
        for copy in copies(pair, pair % 2):
            copy.wait()


def attend(lo, hi, near, own, ahead, across, relay, base, amp, q, k, v, tabs, sofar):
    count = own.shape[0]
    size = v.shape[2] // 2
    keys = 3 * count
    number = hi - lo
    hbm = pl.BlockSpec(memory_space=pl.ANY)
    ins = [VMEM] * (9 + len(tabs) + len(relay))
    return pl.pallas_call(
        functools.partial(attend_kernel, lo, number, size, bool(relay)),
        name="attend_heads",
        in_specs=ins + [hbm] * len(sofar),
        out_specs=[hbm] * 2,
        out_shape=[jax.ShapeDtypeStruct(own.shape, BF16)] * 2,
        scratch_shapes=[
            pltpu.VMEM((2, 2, 4 * count, size), BF16),
            pltpu.VMEM((2, 2, 4 * count, size), BF16),
            pltpu.VMEM((4 * count, size), BF16),
            pltpu.VMEM((2, 2, 4 * count, size), BF16),
            pltpu.VMEM((2, count, 2 * size), BF16),
            pltpu.VMEM((2, count, 2 * size), BF16),
            pltpu.SemaphoreType.DMA((2, 2)),
        ],
        input_output_aliases={len(ins) + i: i for i in range(len(sofar))},
        compiler_params=pltpu.CompilerParams(vmem_limit_bytes=LIMIT),
        cost_estimate=pl.CostEstimate(
            flops=number * (20 * count * size * size + 8 * count * keys * size),
            bytes_accessed=12 * count * number * size + 10 * number * size * size,
            transcendentals=2 * number * count * keys,
        ),
    )(near, own, ahead, across, base, amp, q, k, v, *tabs, *relay, *sofar)


def body(hidden, q_weight, k_weight, v_weight, mod_base, mod_amp, levels, steps_table, group_pos):
    count, local_width = hidden.shape
    local_heads, size = q_weight.shape[1], q_weight.shape[2]
    length = lax.axis_size("queue")
    width = local_width * lax.axis_size("tp")
    everyone = range(length)
    base = mod_base[0][:, None, :]
    amp = mod_amp[0][:, None, :]

    cuts = [0, 2 * max(1, int(local_heads // 2 * FIRST)), local_heads]
    *pieces, rows, sums = split(hidden, cuts, size)
    swap = [(i, i ^ 1) for i in everyone]
    two_on = [(i, i + 2) for i in everyone]
    both_ways = [(i, i - 2 if i % 2 else i + 2) for i in everyone]
    near, ahead, across, more = [], [], [], []
    for c, piece in enumerate(pieces):
        near.append(send(piece, swap, length))
        if c < CHUNKS - 1 or length % 2:
            ahead.append(send(piece, two_on, length))
            across.append(send(near[c], both_ways, length))
            more.append(())
        else:
            ahead.append(send(piece, two_on[1::2], length))
            across.append(send(near[c], both_ways[1::2], length))
            even = send(piece, two_on[0::2], length)
            more.append((even, send(ahead[c], swap, length)))

    peer = other_core(sums)
    squares = token_squares(rows, sums, peer, levels, steps_table, base, amp, q_weight, k_weight, width)
    total = squares + other_core(squares)
    line = jnp.arange(8, dtype=jnp.int32)[:, None]
    factor = jnp.where(line == 2, math.log2(math.e) / math.sqrt(size), 1.0)
    own_stats = jnp.where((line == 2) | (line == 3), lax.rsqrt(total / width + 1e-06) * factor, squares)
    stats = [
        send(own_stats, [(i, i + 2) for i in everyone], length, wrap=True),
        send(own_stats, [(i, i + 1) for i in everyone], length, wrap=True),
        own_stats,
        send(own_stats, [(i, i - 1) for i in everyone], length, wrap=True),
    ]
    tabs = tables(stats, group_pos, local_width, count, size)
    q = block_maps(q_weight[0], True)
    k = block_maps(k_weight[0], True)
    v = block_maps(v_weight[0], False)

    outs = ()
    for c, (lo, hi) in enumerate(zip(cuts[:-1], cuts[1:])):
        outs = attend(lo, hi, near[c], rows, ahead[c], across[c], more[c], base, amp, q, k, v, tabs, outs)
    velocity, new_queue = outs
    return (new_queue, velocity)


def solution(mesh):
    return jax.shard_map(
        body,
        mesh=mesh,
        in_specs=(
            P(("groups", "queue"), "tp"),
            P(None, "tp", None, None),
            P(None, "tp", None, None),
            P(None, "tp", None, None),
            P(None, None, "tp"),
            P(None, None, "tp"),
            P(("groups", "queue")),
            P(),
            P("groups"),
        ),
        out_specs=(P(("groups", "queue"), "tp"), P(("groups", "queue"), "tp")),
        check_vma=False,
    )
```

```python
import functools
import math

import jax
import jax.numpy as jnp
from jax import lax
from jax.experimental import pallas as pl
from jax.experimental.pallas import tpu as pltpu
from jax.sharding import PartitionSpec as P

WIDE = 52
HW_DEV = 104
PERIOD = 256
CHUNKS = 2
FIRST = 0.5
SUM_HEADS = 5
LIMIT = 24 << 20
F32 = jnp.float32
BF16 = jnp.bfloat16
VMEM = pl.BlockSpec(memory_space=pltpu.VMEM)
HBM = pl.BlockSpec(memory_space=pltpu.HBM)


def send(array, pairs, length, wrap=False):
    if wrap:
        pairs = [(a, b % length) for a, b in pairs]
    pairs = [(a, b) for a, b in pairs if 0 <= b < length]
    return lax.ppermute(array, "queue", pairs)


def other_core(array):
    if lax.axis_size("tp") == 2:
        return lax.ppermute(array, "tp", [(0, 1), (1, 0)])
    return lax.psum(array, "tp") - array


def in_hbm(array):
    return pltpu.with_memory_space_constraint(array, pltpu.HBM)


def divisor(count, most):
    return max(k for k in range(1, most + 1) if count % k == 0)


def time_embed(moment, channel):
    within = channel % 256
    freq = jnp.exp(-jnp.log(10000.0) * (within % 128).astype(F32) / 128.0)
    angle = moment * freq
    return jnp.where(within < 128, jnp.cos(angle), jnp.sin(angle))


def pair_plan(shape, size):
    half = size // 2
    side = size // 6
    lead = (size - 4 * side) // 2
    pair = lax.broadcasted_iota(jnp.int32, shape, len(shape) - 1) % half
    part = jnp.where(pair < lead, 0, jnp.where(pair < lead + side, 1, 2))
    within = pair - jnp.where(part == 0, 0, jnp.where(part == 1, lead, lead + side))
    pairs = jnp.where(part == 0, lead, side).astype(F32)
    return part, jnp.exp(-math.log(10000.0) * (within.astype(F32) / pairs))


def block_maps(weight, apart):
    heads, size = weight.shape[:2]
    col = jnp.arange(2 * size)[None, :]
    half = size // 2
    if apart:
        source = 2 * (col % half) + col // size
        owner = col % size // half
    else:
        source = col % size
        owner = col // size
    spread = (jnp.arange(size)[:, None] == source).astype(BF16)
    full = jnp.einsum("pde,ef->pdf", weight.reshape(heads // 2, 2 * size, size), spread)
    mine = jnp.arange(2 * size)[:, None] // size == owner
    return jnp.where(mine, full, jnp.zeros_like(full))


def normed_mix(x, mean, rstd, shift, scale):
    return ((x - mean) * rstd * (1.0 + scale) + shift).astype(BF16)


def to_rows(columns, size):
    count = columns[0].shape[0]
    lane = lax.broadcasted_iota(jnp.int32, (count, size), 1)
    wide = jnp.zeros((count, size), F32)
    for j, column in enumerate(columns):
        wide = jnp.where(lane == j, jnp.broadcast_to(column, (count, size)), wide)
    return jnp.transpose(wide)[:8]


def split_kernel(size, cuts, x_hbm, *refs):
    outs, (x_ref, sums_ref, sems) = refs[: len(cuts) - 1], refs[len(cuts) - 1 :]
    count, _ = x_ref.shape
    blocks = []
    for piece, lo, hi in zip(outs, cuts[:-1], cuts[1:]):
        middle = (lo + hi) // 2
        for start, stop in ((lo, middle), (middle, hi)):
            here = slice(start * size, stop * size)
            there = slice((start - lo) * size, (stop - lo) * size)
            i = len(blocks)
            blocks.append(
                (
                    start,
                    stop,
                    pltpu.make_async_copy(x_hbm.at[:, here], x_ref.at[:, here], sems.at[0, i]),
                    pltpu.make_async_copy(x_ref.at[:, here], piece.at[:, there], sems.at[1, i]),
                )
            )
    for *_, come, _ in blocks:
        come.start()
    total = jnp.zeros((count, size), F32)
    second = jnp.zeros((count, size), F32)
    for start, stop, come, go in blocks:
        come.wait()
        go.start()
        for h in range(start, stop):
            x = x_ref[:, h * size : (h + 1) * size].astype(F32)
            total += x
            second += x * x
    sums_ref[...] = to_rows(
        [jnp.sum(total, axis=1, keepdims=True), jnp.sum(second, axis=1, keepdims=True)], size
    )
    for *_, go in blocks:
        go.wait()


def split(x, cuts, size):
    count, width = x.shape
    return pl.pallas_call(
        functools.partial(split_kernel, size, cuts),
        name="token_split",
        in_specs=[HBM],
        out_specs=[HBM] * (len(cuts) - 1) + [VMEM, VMEM],
        out_shape=[jax.ShapeDtypeStruct((count, (hi - lo) * size), BF16) for lo, hi in zip(cuts[:-1], cuts[1:])]
        + [jax.ShapeDtypeStruct(x.shape, BF16), jax.ShapeDtypeStruct((8, count), F32)],
        scratch_shapes=[pltpu.SemaphoreType.DMA((2, 2 * len(cuts) - 2))],
        compiler_params=pltpu.CompilerParams(vmem_limit_bytes=LIMIT),
        cost_estimate=pl.CostEstimate(flops=4 * count * width, bytes_accessed=4 * count * width, transcendentals=0),
    )(in_hbm(x))


def squares_kernel(
    width, level_ref, steps_hbm, x_ref, own_ref, peer_ref, base_hbm, amp_hbm, q_hbm, k_hbm,
    out_ref, acc, tab, emb, steps, base, amp, q_ref, k_ref, sems,
):
    count = x_ref.shape[0]
    local_heads, size = q_ref.shape[:2]
    share = divisor(local_heads, SUM_HEADS)
    small = [
        pltpu.make_async_copy(src, dst, sems.at[i])
        for i, (src, dst) in enumerate(((steps_hbm, steps), (base_hbm, base), (amp_hbm, amp)))
    ]
    large = [
        [
            pltpu.make_async_copy(
                src.at[0, lo : lo + share], dst.at[lo : lo + share], sems.at[3 + 2 * (lo // share) + i]
            )
            for i, (src, dst) in enumerate(((q_hbm, q_ref), (k_hbm, k_ref)))
        ]
        for lo in range(0, local_heads, share)
    ]
    for copy in small + sum(large, []):
        copy.start()
    acc[...] = jnp.zeros_like(acc)
    cols = jnp.transpose(own_ref[...] + peer_ref[...])
    mean = cols[:, 0:1] / width
    rstd = lax.rsqrt(cols[:, 1:2] / width - mean * mean + 1e-06)
    tab[0] = jnp.broadcast_to(mean, (count, size))
    tab[1] = jnp.broadcast_to(rstd, (count, size))
    for copy in small:
        copy.wait()
    moment = [steps[level_ref[0] + i].astype(F32) for i in range(2)]
    first = lax.axis_index("tp") * (width // lax.axis_size("tp"))
    emb[...] = time_embed(moment[0], lax.broadcasted_iota(jnp.int32, emb.shape, 1) + first)
    for h in range(local_heads):
        if h % share == 0:
            for copy in large[h // share]:
                copy.wait()
        cut = slice(h * size, (h + 1) * size)
        off = (h * size) % PERIOD
        mod = lambda i: base[i, :, cut] + amp[i, :, cut] * emb[0:1, off : off + size]
        mixed = normed_mix(x_ref[:, cut].astype(F32), tab[0], tab[1], mod(0), mod(1))
        both = jnp.concatenate([q_ref[h], k_ref[h]], axis=1)
        raw = jnp.dot(mixed, both, preferred_element_type=F32)
        acc[...] += raw * raw
    out_ref[...] = to_rows(
        [
            mean,
            rstd,
            jnp.sum(acc[:, :size], axis=1, keepdims=True),
            jnp.sum(acc[:, size:], axis=1, keepdims=True),
            jnp.full((count, 1), moment[0]),
            jnp.full((count, 1), moment[1]),
        ],
        size,
    )


def token_squares(x, own, peer, levels, steps_table, base, amp, q_weight, k_weight, width):
    count = x.shape[0]
    local_heads, size = q_weight.shape[1], q_weight.shape[2]
    number = local_heads // divisor(local_heads, SUM_HEADS)
    return pl.pallas_call(
        functools.partial(squares_kernel, width),
        name="token_squares",
        in_specs=[pl.BlockSpec(memory_space=pltpu.SMEM), HBM, VMEM, VMEM, VMEM] + [HBM] * 4,
        out_specs=VMEM,
        out_shape=jax.ShapeDtypeStruct((8, count), F32),
        scratch_shapes=[
            pltpu.VMEM((count, 2 * size), F32),
            pltpu.VMEM((2, count, size), F32),
            pltpu.VMEM((8, PERIOD), F32),
            pltpu.SMEM(steps_table.shape, jnp.int32),
            pltpu.VMEM(base.shape, F32),
            pltpu.VMEM(amp.shape, F32),
            pltpu.VMEM(q_weight.shape[1:], BF16),
            pltpu.VMEM(k_weight.shape[1:], BF16),
            pltpu.SemaphoreType.DMA((3 + 2 * number,)),
        ],
        compiler_params=pltpu.CompilerParams(vmem_limit_bytes=LIMIT),
        cost_estimate=pl.CostEstimate(
            flops=4 * count * local_heads * size * size,
            bytes_accessed=2 * count * local_heads * size + 4 * local_heads * size * size,
            transcendentals=0,
        ),
    )(levels, in_hbm(steps_table), x, own, peer, *map(in_hbm, (base, amp, q_weight, k_weight)))


def tables_kernel(
    first, pos_ref, a_ref, swap_ref, own_ref, other_ref,
    mean_ref, rstd_ref, ck_ref, sk_ref, cq_ref, sq_ref, emb_ref, step_ref,
):
    count, size = mean_ref.shape[1:]
    frames = -(-count // HW_DEV)
    position = lax.axis_index("queue")
    last = lax.axis_size("queue") - 1
    inner = lax.broadcasted_iota(jnp.int32, (HW_DEV, size), 0)
    part, freq = pair_plan((HW_DEV, size), size)
    hpos = (inner // WIDE).astype(F32)
    wpos = (inner % WIDE).astype(F32)
    angle = jnp.where(part == 1, hpos, wpos) * freq
    pcos, psin = jnp.cos(angle), jnp.sin(angle)
    row = lax.broadcasted_iota(jnp.int32, (8, size), 0)
    _, ffreq = pair_plan((8, size), size)
    emb_row = lax.broadcasted_iota(jnp.int32, emb_ref.shape, 0)
    moment = jnp.zeros(emb_ref.shape, F32)
    odd = position % 2 == 1
    swapped, other = swap_ref[...], other_ref[...]
    before, after = jnp.where(odd, swapped, other), jnp.where(odd, other, swapped)
    for g, stats in enumerate((a_ref[...], before, own_ref[...], after)):
        start = pos_ref[jnp.clip(position + (g - 2), 0, last)]
        fangle = (start + row).astype(F32) * ffreq
        fcos, fsin = jnp.cos(fangle), jnp.sin(fangle)
        cols = jnp.transpose(stats)
        moment = jnp.where(emb_row == g, stats[4:5, 0:1], moment)
        for f in range(frames):
            lo, hi = f * HW_DEV, min((f + 1) * HW_DEV, count)
            cos = jnp.where(part == 0, fcos[f : f + 1], pcos)[: hi - lo]
            sin = jnp.where(part == 0, fsin[f : f + 1], psin)[: hi - lo]
            column = lambda j: jnp.broadcast_to(cols[lo:hi, j : j + 1], (hi - lo, size))
            mean_ref[g, lo:hi] = column(0)
            rstd_ref[g, lo:hi] = column(1)
            ck_ref[g, lo:hi] = cos * column(3)
            sk_ref[g, lo:hi] = sin * column(3)
            if g in (1, 2):
                cq_ref[g - 1, lo:hi] = cos * column(2)
                sq_ref[g - 1, lo:hi] = sin * column(2)
    channel = lax.broadcasted_iota(jnp.int32, emb_ref.shape, 1) + lax.axis_index("tp") * first
    emb_ref[...] = time_embed(moment, channel)
    step_ref[...] = jnp.broadcast_to((before[5:6, 0:size] - before[4:5, 0:size]) / 1000.0, step_ref.shape)


def tables(stats, group_pos, first, count, size):
    four = jax.ShapeDtypeStruct((4, count, size), F32)
    two = jax.ShapeDtypeStruct((2, count, size), F32)
    return pl.pallas_call(
        functools.partial(tables_kernel, first),
        name="token_tables",
        in_specs=[pl.BlockSpec(memory_space=pltpu.SMEM)] + [VMEM] * 4,
        out_specs=[VMEM] * 8,
        out_shape=[four, four, four, four, two, two]
        + [jax.ShapeDtypeStruct((8, PERIOD), F32), jax.ShapeDtypeStruct((8, size), F32)],
        compiler_params=pltpu.CompilerParams(vmem_limit_bytes=LIMIT),
        cost_estimate=pl.CostEstimate(flops=count * size * 60, bytes_accessed=count * size * 80, transcendentals=0),
    )(group_pos, *stats)


def attend_kernel(
    lo, number, size, relayed,
    near_ref, own_ref, ahead_ref, across_ref, base_ref, amp_ref, q_ref, k_ref, v_ref,
    mean_ref, rstd_ref, ck_ref, sk_ref, cq_ref, sq_ref, emb_ref, step_ref, *rest,
):
    vel_hbm, new_hbm, keys, values, counted, queries, vel_out, new_out, sems = rest[-9:]
    count = own_ref.shape[0]
    two = 2 * size
    first = lo // 2
    position = lax.axis_index("queue")
    odd = position % 2 == 1
    has_b = position > 0
    there = {0: position > 1, 1: has_b, 3: position < lax.axis_size("queue") - 1}
    rows = lambda g: slice(g * count, (g + 1) * count)
    half = (slice(0, size), slice(size, two))

    def lanes(pair, side):
        return pl.ds(pl.multiple_of(pair * two + side * size, size), size)

    def tokens(pair, side, g):
        held = lambda ref: ref[:, lanes(pair, side)]
        if g == 2:
            return own_ref[:, lanes(first + pair, side)].astype(F32)
        if g == 0:
            back = held(ahead_ref)
            if relayed:
                back = jnp.where(odd, back, held(rest[0]))
            return back.astype(F32)
        near, far = held(near_ref), held(across_ref)
        if relayed:
            far = jnp.where(odd, far, held(rest[1]))
        return (jnp.where(odd, near, far) if g == 1 else jnp.where(odd, far, near)).astype(F32)

    def mod(pair, side, g, i):
        off = (side * size) % PERIOD
        cut = lanes(first + pair, side)
        return base_ref[i, :, cut] + amp_ref[i, :, cut] * emb_ref[g : g + 1, off : off + size]

    def mix(pair, g):
        return jnp.concatenate(
            [
                normed_mix(
                    tokens(pair, side, g), mean_ref[g], rstd_ref[g], mod(pair, side, g, 0), mod(pair, side, g, 1)
                )
                for side in range(2)
            ],
            axis=1,
        )

    def turned(raw, cos, sin):
        one, other = raw[:, :size], raw[:, size:]
        return (one * cos - other * sin).astype(BF16), (one * sin + other * cos).astype(BF16)

    def project(pair, slot, g, mixed):
        key = turned(jnp.dot(mixed, k_ref[first + pair], preferred_element_type=F32), ck_ref[g], sk_ref[g])
        raw = jnp.dot(mixed, v_ref[first + pair], preferred_element_type=F32).astype(BF16)
        for i in range(2):
            value = raw[:, half[i]]
            part = key[i]
            if g in there:
                part = jnp.where(there[g], part, keys[slot, i, rows(2)])
                value = jnp.where(there[g], value, jnp.zeros_like(value))
            keys[slot, i, rows(g)] = part
            values[slot, i, rows(g)] = value
        if g in (1, 2):
            raw = jnp.dot(mixed, q_ref[first + pair], preferred_element_type=F32)
            parts = turned(raw, cq_ref[g - 1], sq_ref[g - 1])
            lane = lax.broadcasted_iota(jnp.int32, (1, size), 1)
            for side in range(2):
                mine = (lane < size // 2) == (side == 0)
                for i in range(2):
                    queries[slot, i, rows(2 * (g - 1) + side)] = jnp.where(mine, parts[i], jnp.zeros_like(parts[i]))

    def dot_keys(slot, query_rows, span):
        return lax.dot_general(
            jnp.concatenate([queries[slot, i, query_rows] for i in range(2)], axis=1),
            jnp.concatenate([keys[slot, i, span] for i in range(2)], axis=1),
            (((1,), (1,)), ((), ())),
            preferred_element_type=F32,
        )

    def soften(shared, single):
        top = jnp.maximum(jnp.max(shared, axis=-1, keepdims=True), jnp.max(single, axis=-1, keepdims=True))
        return jnp.exp2(shared - top).astype(BF16), jnp.exp2(single - top).astype(BF16)

    def gather(slot, side, weights):
        wide = lambda span: jnp.concatenate([values[slot, side, span], counted[span]], axis=1)
        common = slice(count, 3 * count)
        total = jnp.dot(
            jnp.concatenate([shared for shared, _ in weights], axis=0), wide(common), preferred_element_type=F32
        )
        outs = []
        for g, own in ((0, 0), (1, 3)):
            part = total[rows(g)] + jnp.dot(weights[g][1], wide(rows(own)), preferred_element_type=F32)
            outs.append(part[:, :size] / part[:, size:])
        return outs

    def finish(pair, slot, side, g, attn):
        x = tokens(pair, side, g + 1)
        state = x + mod(pair, side, g + 1, 2) * attn
        if g == 1:
            vel_out[slot, :, half[side]] = state.astype(BF16)
        else:
            moved = x + step_ref[0:1, :] * state
            new_out[slot, :, half[side]] = jnp.where(has_b, moved, 0.0).astype(BF16)

    def copies(pair, slot):
        to = pl.ds(pl.multiple_of((first + pair) * two, two), two)
        return [
            pltpu.make_async_copy(out.at[slot], hbm.at[:, to], sems.at[i, slot])
            for i, (out, hbm) in enumerate(((vel_out, vel_hbm), (new_out, new_hbm)))
        ]

    def attention(pair, slot, following):
        other = 1 - slot
        if isinstance(pair, int):
            if pair >= 2:
                for copy in copies(pair - 2, slot):
                    copy.wait()
        else:
            @pl.when(pair >= 2)
            def _():
                for copy in copies(pair - 2, slot):
                    copy.wait()

        shared = dot_keys(slot, slice(0, 4 * count), slice(count, 3 * count))
        single = [
            dot_keys(slot, slice(0, 2 * count), rows(0)),
            dot_keys(slot, slice(2 * count, 4 * count), rows(3)),
        ]
        for side, groups in ((0, (2, 1)), (1, (0, 3))):
            if following:
                mixed = [mix(pair + 1, j) for j in groups]
            weights = [soften(shared[rows(2 * g + side)], single[g][rows(side)]) for g in range(2)]
            if following:
                for j, m in zip(groups, mixed):
                    project(pair + 1, other, j, m)
            for g, total in enumerate(gather(slot, side, weights)):
                finish(pair, slot, side, g, total)
        for copy in copies(pair, slot):
            copy.start()

    pairs = number // 2
    for g in range(4):
        ones = jnp.ones((count, size), BF16)
        if g in there:
            ones = jnp.where(there[g], ones, jnp.zeros_like(ones))
        counted[rows(g)] = ones
    for g in (2, 1, 0, 3):
        project(0, 0, g, mix(0, g))
    looped = (pairs - 1) // 2

    def step(i, _):
        attention(2 * i, 0, True)
        attention(2 * i + 1, 1, True)

    lax.fori_loop(0, looped, step, None)
    for pair in range(2 * looped, pairs):
        attention(pair, pair % 2, pair < pairs - 1)
    for pair in range(max(0, pairs - 2), pairs):
        for copy in copies(pair, pair % 2):
            copy.wait()


def attend(lo, hi, near, own, ahead, across, relay, base, amp, q, k, v, tabs, sofar):
    count = own.shape[0]
    size = v.shape[2] // 2
    keys = 3 * count
    number = hi - lo
    hbm = pl.BlockSpec(memory_space=pl.ANY)
    ins = [VMEM] * (9 + len(tabs) + len(relay))
    return pl.pallas_call(
        functools.partial(attend_kernel, lo, number, size, bool(relay)),
        name="attend_heads",
        in_specs=ins + [hbm] * len(sofar),
        out_specs=[hbm] * 2,
        out_shape=[jax.ShapeDtypeStruct(own.shape, BF16)] * 2,
        scratch_shapes=[
            pltpu.VMEM((2, 2, 4 * count, size), BF16),
            pltpu.VMEM((2, 2, 4 * count, size), BF16),
            pltpu.VMEM((4 * count, size), BF16),
            pltpu.VMEM((2, 2, 4 * count, size), BF16),
            pltpu.VMEM((2, count, 2 * size), BF16),
            pltpu.VMEM((2, count, 2 * size), BF16),
            pltpu.SemaphoreType.DMA((2, 2)),
        ],
        input_output_aliases={len(ins) + i: i for i in range(len(sofar))},
        compiler_params=pltpu.CompilerParams(vmem_limit_bytes=LIMIT),
        cost_estimate=pl.CostEstimate(
            flops=number * (20 * count * size * size + 8 * count * keys * size),
            bytes_accessed=12 * count * number * size + 10 * number * size * size,
            transcendentals=2 * number * count * keys,
        ),
    )(near, own, ahead, across, base, amp, q, k, v, *tabs, *relay, *sofar)


def body(hidden, q_weight, k_weight, v_weight, mod_base, mod_amp, levels, steps_table, group_pos):
    count, local_width = hidden.shape
    local_heads, size = q_weight.shape[1], q_weight.shape[2]
    length = lax.axis_size("queue")
    width = local_width * lax.axis_size("tp")
    everyone = range(length)
    base = mod_base[0][:, None, :]
    amp = mod_amp[0][:, None, :]

    cuts = [0, 2 * max(1, int(local_heads // 2 * FIRST)), local_heads]
    *pieces, rows, sums = split(hidden, cuts, size)
    swap = [(i, i ^ 1) for i in everyone]
    two_on = [(i, i + 2) for i in everyone]
    both_ways = [(i, i - 2 if i % 2 else i + 2) for i in everyone]
    near, ahead, across, more = [], [], [], []
    for c, piece in enumerate(pieces):
        near.append(send(piece, swap, length))
        if c < CHUNKS - 1 or length % 2:
            ahead.append(send(piece, two_on, length))
            across.append(send(near[c], both_ways, length))
            more.append(())
        else:
            ahead.append(send(piece, two_on[1::2], length))
            across.append(send(near[c], both_ways[1::2], length))
            even = send(piece, two_on[0::2], length)
            more.append((even, send(ahead[c], swap, length)))

    peer = other_core(sums)
    squares = token_squares(rows, sums, peer, levels, steps_table, base, amp, q_weight, k_weight, width)
    total = squares + other_core(squares)
    line = jnp.arange(8, dtype=jnp.int32)[:, None]
    factor = jnp.where(line == 2, math.log2(math.e) / math.sqrt(size), 1.0)
    own_stats = jnp.where((line == 2) | (line == 3), lax.rsqrt(total / width + 1e-06) * factor, squares)
    stats = [
        send(own_stats, [(i, i + 2) for i in everyone], length, wrap=True),
        send(own_stats, swap, length),
        own_stats,
        send(own_stats, [(i, i + 1 if i % 2 else i - 1) for i in everyone], length, wrap=length % 2 == 0),
    ]
    tabs = tables(stats, group_pos, local_width, count, size)
    q = block_maps(q_weight[0], True)
    k = block_maps(k_weight[0], True)
    v = block_maps(v_weight[0], False)

    outs = ()
    for c, (lo, hi) in enumerate(zip(cuts[:-1], cuts[1:])):
        outs = attend(lo, hi, near[c], rows, ahead[c], across[c], more[c], base, amp, q, k, v, tabs, outs)
    velocity, new_queue = outs
    return (new_queue, velocity)


def solution(mesh):
    return jax.shard_map(
        body,
        mesh=mesh,
        in_specs=(
            P(("groups", "queue"), "tp"),
            P(None, "tp", None, None),
            P(None, "tp", None, None),
            P(None, "tp", None, None),
            P(None, None, "tp"),
            P(None, None, "tp"),
            P(("groups", "queue")),
            P(),
            P("groups"),
        ),
        out_specs=(P(("groups", "queue"), "tp"), P(("groups", "queue"), "tp")),
        check_vma=False,
    )
```
